32 devices in a mesh: row: 8 (over z, x), col: 4 (over y, core).
Axes of the slice: x: 2, y: 2, z: 4, core: 2. Of those that a mesh axis runs over, the one named last changes fastest.
Arguments:
- charge_drive: float32 [128, 16, 128], P(('row', 'col')), may hold values from -6 to 6
- hardness: float32 [128, 128], P(('row', 'col')), may hold values from 1 to 4
- bond_stiffness: float32 [256, 128], P('row'), may hold values from 0.5 to 4
- coulomb_tiles: float32 [4096, 128, 128], P(('row', 'col')), may hold values from -0.01 to 0.01
- tile_rows: int32 [4096], P(('row', 'col')), may hold values from 0 to 31
- tile_cols: int32 [4096], P(('row', 'col')), may hold values from 0 to 15
- tile_count: int32 [32], P(('row', 'col')), may hold values from 25 to 128, as said below
- link_bonds: int32 [1024], P(('row', 'col')), may hold values from 0 to 31, as said below
- link_cells: int32 [1024], P(('row', 'col')), may hold values from 0 to 31
- link_ends: int32 [1024, 2, 128], P(('row', 'col')), may hold values from 0 to 127, as said below
- link_carry: int32 [1024, 128], P(('row', 'col')), may hold values from 0 to 1, as said below
- link_count: int32 [32], P(('row', 'col')), may hold values from 8 to 32, as said below
Outputs:
- solution: float32 [256, 16, 128], P(('row', 'col'))
- residual: float32 [256, 16, 128], P(('row', 'col'))
The draws below stay inside these ranges and needn't reach their ends.
Inputs may be any that keep to these rules, and one draw needn't show every extreme that they name: `tile_count`: live tile slots of each device, the busiest device has exactly 128. `link_count`: live incidence slots of each device, the busiest device has exactly 32. `link_bonds`: within each row of devices, every bond of every one of the row's bond blocks is carried by exactly one live incidence slot. `link_carry`: dead slots carry nothing. `link_ends`: the two ends of every bond are distinct atoms.
All inputs are finite; a program needn't handle non-finite values.
Results may differ from the reference program's by a relative error of at most 0.00022.
Values sent between devices are 32-bit elements; how exact they have to be, the bound alone decides.
A program may use at most 64 MiB of HBM per device.

```python
import math
import jax
import jax.numpy as jnp
from jax import lax

CELLS_DEV = 4
SETS = 16
CELL_ATOMS = 128
ITERS = 2
GRID_COLS = 4
OWNERS = 32
TILE_SLOTS = 128
LINK_SLOTS = 32
R_CELLS = 32
C_CELLS = 16
ROW_BONDS = 32
NCELLS = 128
NBONDS = 256


def skewed_counts(key, slots, widest):
    first_key, second_key = jax.random.split(key)
    divisor = jax.random.randint(first_key, (OWNERS,), 1, widest + 1)
    counts = slots // divisor
    busiest = jax.random.randint(second_key, (), 0, OWNERS)
    return counts.at[busiest].set(slots).astype(jnp.int32)


def link_layout(key):
    counts = skewed_counts(jax.random.fold_in(key, 23), LINK_SLOTS, 4)
    group_rows = OWNERS // GRID_COLS
    slot_grid = counts.reshape(group_rows, GRID_COLS)
    before = jnp.cumsum(slot_grid, axis=1) - slot_grid
    slot_ids = jnp.arange(LINK_SLOTS, dtype=jnp.int32)
    row_order = (before[:, :, None] + slot_ids[None, None, :]).reshape(group_rows, GRID_COLS * LINK_SLOTS)
    alive_slots = (slot_ids[None, None, :] < slot_grid[:, :, None]).reshape(group_rows, GRID_COLS * LINK_SLOTS)
    live_total = jnp.sum(slot_grid, axis=1)
    position = row_order % ROW_BONDS
    rank_in_block = row_order // ROW_BONDS
    row_keys = jax.random.split(jax.random.fold_in(key, 29), group_rows)
    shuffles = jax.vmap(lambda sub_key: jax.random.permutation(sub_key, ROW_BONDS))(row_keys)
    blocks = jax.vmap(lambda table, where: table[where])(shuffles, position)
    block_ids = jnp.arange(ROW_BONDS, dtype=jnp.int32)
    holders = (live_total[:, None] - block_ids[None, :] - 1) // ROW_BONDS + 1
    holder_picks = jax.random.randint(jax.random.fold_in(key, 31), (group_rows, ROW_BONDS, CELL_ATOMS), 0, holders[:, :, None])
    chosen = jax.vmap(lambda table, where: table[where])(holder_picks, position)
    carried = (chosen == rank_in_block[:, :, None]) & alive_slots[:, :, None]
    carried = carried.astype(jnp.int32).reshape(OWNERS * LINK_SLOTS, CELL_ATOMS)
    return (counts, blocks.reshape(OWNERS * LINK_SLOTS).astype(jnp.int32), carried)


def draw_tile_count(key, part):
    return skewed_counts(jax.random.fold_in(key, 11), TILE_SLOTS, 5)


def draw_link_count(key, part):
    return link_layout(key)[0]


def draw_link_bonds(key, part):
    return link_layout(key)[1]


def draw_link_carry(key, part):
    return link_layout(key)[2]


def draw_link_ends(key, part):
    first_key, second_key = jax.random.split(jax.random.fold_in(key, 37))
    gainer = jax.random.randint(first_key, (OWNERS * LINK_SLOTS, CELL_ATOMS), 0, CELL_ATOMS)
    offset = jax.random.randint(second_key, (OWNERS * LINK_SLOTS, CELL_ATOMS), 1, CELL_ATOMS)
    loser = (gainer + offset) % CELL_ATOMS
    return jnp.stack([gainer, loser], axis=1).astype(jnp.int32)


def place_ends(drawn, stream_key, least, top_value):
    longest = drawn.shape.index(max(drawn.shape))
    spots = []
    for shift in (0, 1):
        where = [jax.random.randint(jax.random.fold_in(stream_key, axis), (), 0, length) for axis, length in enumerate(drawn.shape)]
        where[longest] = (where[longest] + shift) % drawn.shape[longest]
        spots.append(tuple(where))
    return drawn.at[spots[0]].set(least).at[spots[1]].set(top_value)


def steps_of(key, extent, cuts, smallest, top_value):
    gain, own = 1.0, jax.random.fold_in(key, 6)
    for axis_at, shards_of in cuts:
        draws = jnp.exp(jax.random.uniform(jax.random.fold_in(own, axis_at), (shards_of,), jnp.float32, smallest / len(cuts), top_value / len(cuts)))
        gain = gain * jnp.repeat(draws, extent[axis_at] // shards_of).reshape([-1 if axis == axis_at else 1 for axis in range(len(extent))])
    return gain


def bell_draw(rng, dims, deviation, reach, pieces=(), kind=jnp.bfloat16):
    level = steps_of(rng, dims, pieces, -0.22, 0.18) if pieces else 1.0
    values = jax.random.normal(rng, dims, jnp.float32) * deviation * level
    return jnp.minimum(jnp.maximum(values, -reach), reach).astype(kind)


def setup_inputs(seed: int = 0) -> dict:
    key_list = jax.random.split(jax.random.key(seed), 13)
    charge_drive = bell_draw(key_list[0], (NCELLS, SETS, CELL_ATOMS), 1.0, 6.0, ((0, 32),), jnp.float32)
    hardness = jnp.clip(jnp.exp(math.log(4.0) - 1.3862944 * jax.random.uniform(key_list[1], (NCELLS, CELL_ATOMS), jnp.float32) ** steps_of(key_list[1], (NCELLS, CELL_ATOMS), ((0, 32),), -0.2, 0.2)), 1.0, 4.0)
    bond_stiffness = jnp.clip(jnp.exp(math.log(4.0) - 2.0794415 * jax.random.uniform(key_list[2], (NBONDS, CELL_ATOMS), jnp.float32) ** steps_of(key_list[2], (NBONDS, CELL_ATOMS), ((0, 8),), -0.2, 0.2)), 0.5, 4.0)
    coulomb_tiles = jnp.clip(jax.random.uniform(key_list[3], (OWNERS * TILE_SLOTS, CELL_ATOMS, CELL_ATOMS), jnp.float32, -0.01, 0.01) * steps_of(key_list[3], (OWNERS * TILE_SLOTS, CELL_ATOMS, CELL_ATOMS), ((0, 32),), -0.4, 0.0), -0.01, 0.01)
    tile_rows = place_ends(jax.random.randint(key_list[4], (OWNERS * TILE_SLOTS,), 0, R_CELLS), jax.random.fold_in(key_list[4], 1), 0, R_CELLS - 1).astype(jnp.int32)
    tile_cols = place_ends(jax.random.randint(key_list[5], (OWNERS * TILE_SLOTS,), 0, C_CELLS), jax.random.fold_in(key_list[5], 1), 0, C_CELLS - 1).astype(jnp.int32)
    tile_count = draw_tile_count(jax.random.fold_in(key_list[12], 71), 0)
    link_bonds = draw_link_bonds(jax.random.fold_in(key_list[12], 71), 0)
    link_cells = place_ends(jax.random.randint(key_list[8], (OWNERS * LINK_SLOTS,), 0, R_CELLS), jax.random.fold_in(key_list[8], 1), 0, R_CELLS - 1).astype(jnp.int32)
    link_ends = draw_link_ends(jax.random.fold_in(key_list[12], 71), 0)
    link_carry = draw_link_carry(jax.random.fold_in(key_list[12], 71), 0)
    link_count = draw_link_count(jax.random.fold_in(key_list[12], 71), 0)
    return {"charge_drive": charge_drive, "hardness": hardness, "bond_stiffness": bond_stiffness, "coulomb_tiles": coulomb_tiles, "tile_rows": tile_rows, "tile_cols": tile_cols, "tile_count": tile_count, "link_bonds": link_bonds, "link_cells": link_cells, "link_ends": link_ends, "link_carry": link_carry, "link_count": link_count}


highest = lax.Precision.HIGHEST


def reference(charge_drive, hardness, bond_stiffness, coulomb_tiles, tile_rows, tile_cols, tile_count, link_bonds, link_cells, link_ends, link_carry, link_count):
    total_cells = hardness.shape[0]
    total_bonds = bond_stiffness.shape[0]
    tile_slot = jnp.arange(coulomb_tiles.shape[0], dtype=jnp.int32)
    tile_owner = tile_slot // TILE_SLOTS
    tile_live = ((tile_slot % TILE_SLOTS) < tile_count[tile_owner]).astype(jnp.float32)
    tile_grid_row = tile_owner // GRID_COLS
    tile_grid_col = tile_owner % GRID_COLS
    target_cell = ((tile_rows // CELLS_DEV) * GRID_COLS + tile_grid_col) * CELLS_DEV + tile_rows % CELLS_DEV
    source_cell = (tile_grid_row * GRID_COLS + tile_cols // CELLS_DEV) * CELLS_DEV + tile_cols % CELLS_DEV
    link_slot = jnp.arange(link_bonds.shape[0], dtype=jnp.int32)
    link_owner = link_slot // LINK_SLOTS
    link_live = ((link_slot % LINK_SLOTS) < link_count[link_owner]).astype(jnp.float32)
    link_grid_row = link_owner // GRID_COLS
    link_grid_col = link_owner % GRID_COLS
    link_cell_global = ((link_cells // CELLS_DEV) * GRID_COLS + link_grid_col) * CELLS_DEV + link_cells % CELLS_DEV
    link_bond_global = link_grid_row * ROW_BONDS + link_bonds
    atom_ids = jnp.arange(128, dtype=jnp.int32)
    incidence = ((link_ends[:, 0, :, None] == atom_ids).astype(jnp.float32)
                 - (link_ends[:, 1, :, None] == atom_ids).astype(jnp.float32))
    incidence = incidence * link_live[:, None, None] * link_carry.astype(jnp.float32)[:, :, None]

    def bond_to_charge(bonds):
        parts = jnp.einsum("sba,sxb->sxa", incidence, bonds[link_bond_global], precision=highest)
        return jax.ops.segment_sum(parts, link_cell_global, num_segments=total_cells)

    def charge_to_bond(potential):
        parts = jnp.einsum("sba,sxa->sxb", incidence, potential[link_cell_global], precision=highest)
        return jax.ops.segment_sum(parts, link_bond_global, num_segments=total_bonds)

    def coulomb(charge):
        products = jnp.einsum("tij,txj->txi", coulomb_tiles, charge[source_cell], precision=highest)
        products = products * tile_live[:, None, None]
        mirrored = jnp.einsum("tij,txi->txj", coulomb_tiles, charge[target_cell], precision=highest)
        mirrored = mirrored * tile_live[:, None, None]
        return (hardness[:, None, :] * charge
                + jax.ops.segment_sum(products, target_cell, num_segments=total_cells)
                + jax.ops.segment_sum(mirrored, source_cell, num_segments=total_cells))

    def operate(direction):
        return charge_to_bond(coulomb(bond_to_charge(direction))) + bond_stiffness[:, None, :] * direction

    def totals(values):
        return jnp.sum(values, axis=(0, 2))

    right_side = -charge_to_bond(charge_drive)
    solution = jnp.zeros_like(right_side)
    residual = right_side
    direction = right_side
    norm_now = totals(residual * residual)
    for iteration in range(ITERS):
        applied = operate(direction)
        step_size = (norm_now / totals(direction * applied))[None, :, None]
        solution = solution + step_size * direction
        residual = residual - step_size * applied
        norm_next = totals(residual * residual)
        direction = residual + (norm_next / norm_now)[None, :, None] * direction
        norm_now = norm_next
    return solution, residual
```

```python
import functools

import jax
import jax.numpy as jnp
from jax import lax
from jax.experimental import pallas as pl
from jax.experimental.pallas import tpu as pltpu
from jax.sharding import PartitionSpec as P

MESH = pl.DeviceIdType.MESH
NT = (((1,), (1,)), ((), ()))
NN = (((1,), (0,)), ((), ()))


def halves(value):
    high = value.astype(jnp.bfloat16)
    low = (value - high.astype(jnp.float32)).astype(jnp.bfloat16)
    return high, low


def dot(left, right, dims=NN):
    return lax.dot_general(left, right, dims, preferred_element_type=jnp.float32)


class Row:
    def __init__(self, rows, send, recv, started):
        self.rows, self.send, self.recv, self.started = rows, send, recv, started
        self.inner = 2 if rows % 2 == 0 else 1
        self.outer = rows // self.inner
        self.r, self.c = lax.axis_index("row"), lax.axis_index("col")
        self.high, self.low = self.r // self.inner, lax.rem(self.r, self.inner)

    def copy(self, phase, index, source, target, peer):
        copy = pltpu.make_async_remote_copy(
            src_ref=source, dst_ref=target,
            send_sem=self.send.at[phase, index], recv_sem=self.recv.at[phase, index],
            device_id=(peer, self.c), device_id_type=MESH,
        )
        copy.start()
        self.started.append(copy)
        return copy

    def near_peer(self):
        return self.high * self.inner + self.inner - 1 - self.low

    def gather_begin(self, phase, source, slot_of):
        far = [
            self.copy(
                phase, k * self.inner, source, slot_of(self.r),
                lax.rem(self.high + k, self.outer) * self.inner + self.low,
            )
            for k in range(1, self.outer)
        ]
        near = [
            self.copy(phase, 1, source, slot_of(self.r), self.near_peer())
            for _ in range(self.inner - 1)
        ]
        return far, near

    def gather_relay(self, phase, copies, slot_of):
        far, near = copies
        for k, copy in enumerate(far, 1):
            copy.wait_recv()
            if self.inner > 1:
                block = slot_of(lax.rem(self.high + self.outer - k, self.outer) * self.inner + self.low)
                near.append(self.copy(phase, k * self.inner + 1, block, block, self.near_peer()))

    def gather_end(self, copies):
        for copy in copies[1]:
            copy.wait_recv()


def greet(rows, cols, r, c, with_cols):
    barrier = pltpu.get_barrier_semaphore()
    for k in range(1, rows):
        pl.semaphore_signal(barrier, inc=1, device_id=(lax.rem(r + k, rows), c), device_id_type=MESH)
    if with_cols:
        for k in range(1, cols):
            pl.semaphore_signal(barrier, inc=1, device_id=(r, lax.rem(c + k, cols)), device_id_type=MESH)
    return barrier


def link_kernel(
    rows, cols, sizes,
    tile_rows, tile_cols, link_bonds, link_cells, tiles_live, links_live, bonds, ends_hbm, carry, stiffness,
    table, ends_all, weight_all, cells_all,
    ids, sem, row_send, row_recv,
):
    link_slots, lanes = carry.shape
    width = ids.shape[1]
    started = []
    row = Row(rows, row_send, row_recv, started)
    r, c = row.r, row.c
    barrier = greet(rows, cols, r, c, False)
    own_ends = pltpu.make_async_copy(ends_hbm, ends_all.at[r], sem.at[2])
    own_ends.start()
    ids[...] = jnp.zeros_like(ids)
    copies = []
    for i, (source, target) in enumerate((
        (tile_rows, ids.at[0:1, 0 : tile_rows.shape[1]]), (tile_cols, ids.at[1:2, 0 : tile_cols.shape[1]]),
    )):
        copy = pltpu.make_async_copy(source, target, sem.at[i])
        copy.start()
        copies.append(copy)
    ids[2:3, 0:link_slots] = link_bonds[...]
    ids[3:4, 0:link_slots] = link_cells[...]
    tile_count, link_count = tiles_live[0], links_live[0]
    slot = lax.broadcasted_iota(jnp.int32, (8, width), 1)
    cells_all[r] = jnp.where(slot < link_count, jnp.broadcast_to(ids[3:4, :], (8, width)), -1)
    for s in range(link_slots):
        live = jnp.full((1, lanes), s, jnp.int32) < link_count
        kept = jnp.where(live, carry[s : s + 1, :], 0).astype(jnp.float32)
        weight_all[r, s : s + 1, :] = kept * stiffness[pl.ds(bonds[0, s], 1), :]
    slots = (lambda i: ends_all.at[i]), (lambda i: weight_all.at[i]), (lambda i: cells_all.at[i])
    pl.semaphore_wait(barrier, rows - 1)
    gathers = [
        row.gather_begin(phase, ends_hbm if phase == 0 else of(r), of) for phase, of in enumerate(slots)
    ]
    for copy in copies:
        copy.wait()
    beyond = 1 << 20
    down = lax.broadcasted_iota(jnp.int32, (width, width), 0)
    across = lax.broadcasted_iota(jnp.int32, (width, width), 1)

    def total(value, axis):
        return jnp.sum(value, axis=axis, keepdims=True)

    def column(value):
        return total(jnp.where(down == across, value, 0), 1)

    for place, (key_row, other, count) in enumerate((
        (0, 1, tile_count), (1, 0, tile_count), (3, 3, link_count), (2, 2, link_count),
    )):
        key = jnp.where(across[0:1] < count, ids[key_row : key_row + 1, :], beyond)
        mine = column(key)
        equal_before = total(jnp.where((key == mine) & (across < down), 1, 0), 1)
        rank = total(jnp.where(key < mine, 1, 0), 1) + equal_before
        here = rank == across
        upto = total(jnp.where(mine <= across, 1, 0), 0)
        fewer = total(jnp.where(mine < across, 1, 0), 0)
        at = 5 * place
        table[at : at + 1, :] = total(jnp.where(here, down, 0), 0)
        table[at + 1 : at + 2, :] = total(jnp.where(here & (equal_before > 0), 1, 0), 0)
        table[at + 2 : at + 3, :] = jnp.maximum(upto - 1, 0)
        table[at + 3 : at + 4, :] = jnp.where(upto > fewer, 1, 0)
        table[at + 4 : at + 5, :] = total(jnp.where(here, column(ids[other : other + 1, :]), 0), 0)
    table[20:22, :] = ids[2:4, :]
    table[22:24, :] = jnp.full((2, width), link_count, jnp.int32)
    own_ends.wait()
    for phase, of in enumerate(slots):
        row.gather_relay(phase, gathers[phase], of)
    for gather in gathers:
        row.gather_end(gather)
    for copy in started:
        copy.wait_send()


GROUP = 4


def cell_kernel(
    rows, sizes, cells, ends_all, weight_all, drive, square_out, charge_out, fixed_out, sums_out, listed, acc,
):
    cells_dev, sets, lanes, link_slots = sizes
    first = lax.axis_index("row") * cells_dev
    acc[...] = jnp.zeros_like(acc)

    def collect(i, found):
        for s in range(link_slots):
            local = cells[i, s] - first
            listed[found] = (i * link_slots + s) * cells_dev + local
            found = found + jnp.where((local >= 0) & (local < cells_dev), 1, 0)
        return found

    found = lax.fori_loop(0, rows, collect, jnp.int32(0))
    for e in range(GROUP):
        listed[found + e] = 0
    atom = lax.broadcasted_iota(jnp.int32, (lanes, lanes), 0)

    def visit(g, sums):
        norm, energy = sums
        for e in range(GROUP):
            i = g * GROUP + e
            code = listed[i]
            s, l = code // cells_dev, lax.rem(code, cells_dev)
            real = jnp.full((1, lanes), i, jnp.int32) < found
            pair = ends_all[s]
            weight = jnp.where(real, weight_all[pl.ds(s, 1), :], 0.0)
            kept = jnp.where(weight != 0.0, 1.0, 0.0)
            gain = jnp.where(atom == pair[0:1, :], kept, 0.0)
            lose = jnp.where(atom == pair[1:2, :], kept, 0.0)
            matrix = (gain - lose).astype(jnp.bfloat16)
            high, low = halves(drive[l])
            both = dot(jnp.concatenate([high, low], axis=0), matrix)
            u = -(both[0:sets] + both[sets : 2 * sets])
            ku = weight * u
            norm = norm + u * u
            energy = energy + ku * u
            left = jnp.concatenate([matrix, *halves(u), *halves(ku)], axis=0)
            acc[l] += dot(left, matrix, NT)
        return norm, energy

    zero = jnp.zeros((sets, lanes), jnp.float32)
    norm, energy = lax.fori_loop(0, (found + GROUP - 1) // GROUP, visit, (zero, zero))
    sums_out[0] = norm
    sums_out[1] = energy
    for l in range(cells_dev):
        high, low = halves(acc[l, 0:lanes, :])
        square_out[l, :, 0:lanes] = high
        square_out[l, :, lanes : 2 * lanes] = low
        at = lanes
        charge_out[l] = acc[l, at : at + sets, :] + acc[l, at + sets : at + 2 * sets, :]
        at = lanes + 2 * sets
        fixed_out[l] = acc[l, at : at + sets, :] + acc[l, at + sets : at + 2 * sets, :]


def kernel(
    rows, cols, sizes,
    table, drive, hardness_hbm, stiffness_hbm, tiles_hbm, ends_hbm, carry_hbm, square, charge0, fixed, sums0,
    out_solution, out_residual,
    hardness, stiffness, ends, carry,
    tiles, tile_parts, incidence, u0, u1, u2, products, bond_products,
    drive_all, row_charge, col_charge,
    row_parts, col_parts, pot_part, pot_in, mirror_part, mirror_in, pot_all, pot_parts,
    bond_part, bond_in, dots_row, dots_col,
    small_sem, tile_sem, row_send, row_recv, col_send, col_recv,
):
    cells_dev, sets, lanes, tile_slots, link_slots, row_bonds = sizes
    group_cells, row_cells = rows * cells_dev, cols * cells_dev
    share = row_bonds // cols
    block = cells_dev * sets
    started = []
    row = Row(rows, row_send, row_recv, started)
    r, c = row.r, row.c

    small = []
    for i, (source, target) in enumerate((
        (ends_hbm, ends), (carry_hbm, carry),
        (hardness_hbm, hardness), (stiffness_hbm, stiffness), (drive, drive_all.at[r]),
    )):
        copy = pltpu.make_async_copy(source, target, small_sem.at[i])
        copy.start()
        small.append(copy)
    barrier = greet(rows, cols, r, c, True)
    chunks = tile_sem.shape[0]
    per_chunk = tile_slots // chunks
    tile_copies = []
    for i in range(chunks):
        part = pl.ds(i * per_chunk, per_chunk)
        copy = pltpu.make_async_copy(tiles_hbm.at[part], tiles.at[part], tile_sem.at[i])
        copy.start()
        tile_copies.append(copy)
    for l in range(cells_dev):
        part = slice(l * sets, (l + 1) * sets)
        col_charge[0, r, part, :] = charge0[l]
        row_charge[0, c, part, :] = charge0[l]
    link_count = table[22, 0]
    small[0].wait()
    small[1].wait()

    def build_incidence(s, _):
        atom = lax.broadcasted_iota(jnp.int32, (lanes, lanes), 0)
        pair = ends[s]
        live = jnp.full((1, lanes), s, jnp.int32) < link_count
        kept = jnp.where(live, carry[pl.ds(s, 1), :], 0).astype(jnp.float32)
        gain = jnp.where(atom == pair[0:1, :], kept, 0.0)
        lose = jnp.where(atom == pair[1:2, :], kept, 0.0)
        incidence[s] = (gain - lose).astype(jnp.bfloat16)
        return 0

    lax.fori_loop(0, link_slots, build_incidence, 0)
    pl.semaphore_wait(barrier, rows + cols - 2)

    def send_row(phase, source, target):
        return [
            row.copy(phase, k, source(lax.rem(r + k, rows)), target, lax.rem(r + k, rows))
            for k in range(1, rows)
        ]

    def send_col(phase, source, target):
        copies = []
        for k in range(1, cols):
            peer = lax.rem(c + k, cols)
            copy = pltpu.make_async_remote_copy(
                src_ref=source(peer), dst_ref=target,
                send_sem=col_send.at[phase, k], recv_sem=col_recv.at[phase, k],
                device_id=(r, peer), device_id_type=MESH,
            )
            copy.start()
            copies.append(copy)
        started.extend(copies)
        return copies

    def arrive(copies):
        for copy in copies:
            copy.wait_recv()

    def split_tiles(t, _):
        high, low = halves(tiles[t])
        tile_parts[t, 0:lanes, :] = high
        tile_parts[t, lanes : 2 * lanes, :] = low
        return 0

    UNROLL = 32

    def slot(s):
        return pl.ds(pl.multiple_of(s * sets, sets), sets)

    def add_slots(place, value, running, carried, start, stop):
        def body(i, carried):
            for j in range(UNROLL):
                k = i * UNROLL + j
                kept = jnp.full((sets, lanes), table[5 * place + 1, k], jnp.int32).astype(jnp.float32)
                carried = carried * kept + value(k, table[5 * place, k], table[5 * place + 4, k])
                running[k] = carried
            return carried

        return lax.fori_loop(start // UNROLL, stop // UNROLL, body, carried)

    def spread_slots(place, size, running, target):
        def spread(i, _):
            for j in range(4):
                l = i * 4 + j
                some = jnp.full((sets, lanes), table[5 * place + 3, l], jnp.int32).astype(jnp.float32)
                found = running[table[5 * place + 2, l]]
                target[slot(l), :] = found * some
            return 0

        lax.fori_loop(0, size // 4, spread, 0)

    nothing = jnp.zeros((sets, lanes), jnp.float32)

    def to_bonds(potential_of, update):
        def fill(l, _):
            high, low = halves(potential_of(l))
            pot_parts[l, 0:sets, :] = high
            pot_parts[l, sets : 2 * sets, :] = low
            return 0

        lax.fori_loop(0, group_cells, fill, 0)

        def body(i, _):
            for j in range(UNROLL):
                s = i * UNROLL + j
                both = dot(pot_parts[table[21, s]], incidence[s])
                update(s, both[0:sets] + both[sets : 2 * sets])
            return 0

        lax.fori_loop(0, link_slots // UNROLL, body, 0)

    def send_bonds(n, u):
        add_slots(3, lambda k, s, _: u[s], bond_products, nothing, 0, link_slots)
        spread_slots(3, row_bonds, bond_products, bond_part.at[n])
        size = share * sets
        copies = send_col(
            4 + n,
            lambda peer: bond_part.at[n, pl.ds(pl.multiple_of(peer * size, size), size)],
            bond_in.at[n, c],
        )
        bond_in[n, c] = bond_part[n, pl.ds(pl.multiple_of(c * size, size), size), :]
        return copies

    def row_block(peer):
        return pl.ds(pl.multiple_of(peer * block, block), block)

    def drive_slot(i):
        return drive_all.at[i]

    def operate(n, background, prepare, middle, slack):
        def charge_slot(i):
            return col_charge.at[n, i]

        side = send_col(n, lambda peer: row_charge.at[n, c], row_charge.at[n, c])
        gather = row.gather_begin(3 * n, col_charge.at[n, r], charge_slot)
        copies, other_slot, phase = background()
        prepare()
        arrive(side)
        for k in range(cols):
            for l in range(cells_dev):
                high, low = halves(row_charge[n, k, l * sets : (l + 1) * sets, :])
                row_parts[k * cells_dev + l, 0:sets, :] = high
                row_parts[k * cells_dev + l, sets : 2 * sets, :] = low

        def forward(k, t, cell):
            both = dot(row_parts[cell], tile_parts[t], NT)
            return both[0:sets, 0:lanes] + (
                both[sets : 2 * sets, 0:lanes] + both[0:sets, lanes : 2 * lanes]
            )

        half = tile_slots // (2 * UNROLL) * UNROLL
        carried = add_slots(0, forward, products, nothing, 0, half)
        row.gather_relay(3 * n, gather, charge_slot)
        add_slots(0, forward, products, carried, half, tile_slots)
        spread_slots(0, group_cells, products, pot_part.at[n])
        parts = send_row(3 * n + 1, lambda peer: pot_part.at[n, row_block(peer)], pot_in.at[n, r])
        pot_in[n, r] = pot_part[n, row_block(r), :]
        row.gather_relay(phase, copies, other_slot)
        middle()
        row.gather_end(gather)
        for k in range(rows):
            for l in range(cells_dev):
                high, low = halves(col_charge[n, k, l * sets : (l + 1) * sets, :])
                place = k * cells_dev + l
                col_parts[place, 0:sets, 0:lanes] = high
                col_parts[place, 0:sets, lanes : 2 * lanes] = high
                col_parts[place, sets : 2 * sets, 0:lanes] = low
                col_parts[place, sets : 2 * sets, lanes : 2 * lanes] = jnp.zeros_like(low)

        def backward(k, t, cell):
            both = dot(col_parts[cell], tile_parts[t])
            return both[0:sets] + both[sets : 2 * sets]

        add_slots(1, backward, products, nothing, 0, tile_slots)
        spread_slots(1, row_cells, products, mirror_part.at[n])
        side = send_col(2 + n, lambda peer: mirror_part.at[n, row_block(peer)], mirror_in.at[n, c])
        mirror_in[n, c] = mirror_part[n, row_block(c), :]
        row.gather_end(copies)
        slack()
        arrive(parts)
        total = pot_in[n, 0]
        for k in range(1, rows):
            total = total + pot_in[n, k]
        arrive(side)
        for k in range(cols):
            total = total + mirror_in[n, k]
        own = col_charge[n, r]
        for l in range(cells_dev):
            part = slice(l * sets, (l + 1) * sets)
            pot_all[n, r, part, :] = total[part] + hardness[l : l + 1, :] * own[part]

    def pot_slot(n):
        return lambda i: pot_all.at[n, i]

    def potential(n):
        return lambda l: pot_all[
            n, l // cells_dev, pl.ds(pl.multiple_of(lax.rem(l, cells_dev) * sets, sets), sets), :
        ]

    def own_cells(n, l):
        part = slice(l * sets, (l + 1) * sets)
        return col_charge[n, r, part, :], pot_all[n, r, part, :]

    def packed(a, b):
        a = jnp.sum(a, axis=1, keepdims=True)
        b = jnp.sum(b, axis=1, keepdims=True)
        lane = lax.broadcasted_iota(jnp.int32, (sets, lanes), 1)
        return jnp.where(lane == 0, a, jnp.where(lane == 1, b, 0.0))

    def dots_begin(n, values):
        dots_row[n, r] = values
        return send_row(7 + n, lambda peer: dots_row.at[n, r], dots_row.at[n, r])

    def dots_middle(n, copies):
        arrive(copies)
        total = dots_row[n, 0]
        for k in range(1, rows):
            total = total + dots_row[n, k]
        dots_col[n, c] = total
        return send_col(7 + n, lambda peer: dots_col.at[n, c], dots_col.at[n, c])

    def dots_end(n, copies):
        arrive(copies)
        total = dots_col[n, 0]
        for k in range(1, cols):
            total = total + dots_col[n, k]
        return total[:, 0:1], total[:, 1:2]

    state = {}

    def drive_background():
        return row.gather_begin(2, drive, drive_slot), drive_slot, 2

    def prepare_tiles():
        for copy in small[2:]:
            copy.wait()
        for i in range(chunks):
            tile_copies[i].wait()
            lax.fori_loop(i * per_chunk, (i + 1) * per_chunk, split_tiles, 0)

    def first_bonds():
        def first(s, value):
            u0[s] = -value

        to_bonds(lambda l: drive_all[l // cells_dev, lax.rem(l, cells_dev)], first)
        state["bonds0"] = send_bonds(0, u0)

    operate(0, drive_background, prepare_tiles, lambda: None, first_bonds)

    energy = sums0[1]
    for l in range(cells_dev):
        part = slice(l * sets, (l + 1) * sets)
        charge, value = own_cells(0, l)
        both = dot(jnp.concatenate(halves(value), axis=0), square[l])
        new = both[0:sets, 0:lanes] + (
            both[sets : 2 * sets, 0:lanes] + both[0:sets, lanes : 2 * lanes]
        )
        new = new + fixed[l]
        col_charge[1, r, part, :] = new
        row_charge[1, c, part, :] = new
        energy = energy + charge * value

    def potential_background():
        gather = row.gather_begin(5, pot_all.at[0, r], pot_slot(0))
        state["dots"] = dots_begin(0, packed(sums0[0], energy))
        return gather, pot_slot(0), 5

    def first_dots():
        state["dots"] = dots_middle(0, state["dots"])

    def second_bonds():
        def update(s, value):
            u1[s] = value + stiffness[pl.ds(table[20, s], 1), :] * u0[s]

        to_bonds(potential(0), update)
        state["bonds1"] = send_bonds(1, u1)
        norm, energy = dots_end(0, state["dots"])
        state["norm"], state["step"] = norm, norm / energy

        def body(i, sums):
            a, b = sums
            for j in range(4):
                s = i * 4 + j
                residual = u0[s] - state["step"] * u1[s]
                square_of = residual * residual
                a = a + square_of
                b = b + stiffness[pl.ds(table[20, s], 1), :] * square_of
            return a, b

        state["sums"] = lax.fori_loop(0, link_slots // 4, body, (nothing, nothing))

    operate(1, potential_background, lambda: None, first_dots, second_bonds)
    gather = row.gather_begin(6, pot_all.at[1, r], pot_slot(1))
    norm0, step0 = state["norm"], state["step"]
    norm_part, energy_part = state["sums"]
    for l in range(cells_dev):
        charge, value = own_cells(0, l)
        charge1, value1 = own_cells(1, l)
        energy_part = energy_part + (charge - step0 * charge1) * (value - step0 * value1)
    copies = dots_begin(1, packed(norm_part, energy_part))
    row.gather_relay(6, gather, pot_slot(1))
    copies = dots_middle(1, copies)
    row.gather_end(gather)

    def last(s, value):
        u2[s] = value + stiffness[pl.ds(table[20, s], 1), :] * u1[s]

    to_bonds(potential(1), last)
    bonds2 = send_bonds(2, u2)
    norm1, energy1 = dots_end(1, copies)
    arrive(state["bonds0"])
    arrive(state["bonds1"])
    arrive(bonds2)
    gain = norm1 / norm0
    step1 = norm1 / (energy1 - gain * norm1 / step0)
    for j in range(share):
        part = slice(j * sets, (j + 1) * sets)
        total = []
        for n in range(3):
            value = bond_in[n, 0, part, :]
            for k in range(1, cols):
                value = value + bond_in[n, k, part, :]
            total.append(value)
        residual = total[0] - step0 * total[1]
        applied = total[1] - step0 * total[2]
        out_solution[j] = step0 * total[0] + step1 * (residual + gain * total[0])
        out_residual[j] = residual - step1 * (applied + gain * total[1])
    for copy in started:
        copy.wait_send()


def on_device(
    charge_drive,
    hardness,
    bond_stiffness,
    coulomb_tiles,
    tile_rows,
    tile_cols,
    tile_count,
    link_bonds,
    link_cells,
    link_ends,
    link_carry,
    link_count,
):
    rows, cols = lax.axis_size("row"), lax.axis_size("col")
    cells_dev, sets, lanes = charge_drive.shape
    tile_slots, link_slots = coulomb_tiles.shape[0], link_bonds.shape[0]
    row_bonds = bond_stiffness.shape[0]
    group_cells, row_cells = rows * cells_dev, cols * cells_dev
    share = row_bonds // cols
    block = cells_dev * sets
    f32, bf16, i32 = jnp.float32, jnp.bfloat16, jnp.int32
    vmem = pl.BlockSpec(memory_space=pltpu.VMEM)
    smem = pl.BlockSpec(memory_space=pltpu.SMEM)
    hbm = pl.BlockSpec(memory_space=pltpu.HBM)
    width = -(-max(tile_slots, link_slots, group_cells, row_bonds) // 128) * 128
    bonds = link_bonds.reshape(1, -1)
    table, ends_all, weight_all, cells_all = pl.pallas_call(
        functools.partial(link_kernel, rows, cols, None),
        out_shape=(
            jax.ShapeDtypeStruct((24, width), i32),
            jax.ShapeDtypeStruct((rows, *link_ends.shape), i32),
            jax.ShapeDtypeStruct((rows, link_slots, lanes), f32),
            jax.ShapeDtypeStruct((rows, 8, width), i32),
        ),
        in_specs=[hbm] * 2 + [vmem] * 2 + [smem] * 3 + [hbm] + [vmem] * 2,
        out_specs=(vmem,) * 4,
        scratch_shapes=[
            pltpu.VMEM((8, width), i32),
            pltpu.SemaphoreType.DMA((3,)),
            pltpu.SemaphoreType.DMA((3, rows)),
            pltpu.SemaphoreType.DMA((3, rows)),
        ],
        compiler_params=pltpu.CompilerParams(
            collective_id=1, has_side_effects=True, vmem_limit_bytes=67043328
        ),
    )(
        tile_rows.reshape(1, -1), tile_cols.reshape(1, -1), bonds, link_cells.reshape(1, -1),
        tile_count, link_count, bonds, link_ends, link_carry, bond_stiffness,
    )
    square, charge0, fixed, sums0 = pl.pallas_call(
        functools.partial(cell_kernel, rows, (cells_dev, sets, lanes, link_slots)),
        out_shape=(
            jax.ShapeDtypeStruct((cells_dev, lanes, 2 * lanes), bf16),
            jax.ShapeDtypeStruct((cells_dev, sets, lanes), f32),
            jax.ShapeDtypeStruct((cells_dev, sets, lanes), f32),
            jax.ShapeDtypeStruct((2, sets, lanes), f32),
        ),
        in_specs=[smem] + [vmem] * 3,
        out_specs=(vmem,) * 4,
        scratch_shapes=[
            pltpu.SMEM((rows * link_slots + 2 * GROUP,), i32),
            pltpu.VMEM((cells_dev, lanes + 4 * sets, lanes), f32),
        ],
        compiler_params=pltpu.CompilerParams(vmem_limit_bytes=67043328),
    )(
        cells_all[:, 0, :], ends_all.reshape(rows * link_slots, *link_ends.shape[1:]),
        weight_all.reshape(rows * link_slots, lanes), charge_drive,
    )
    out = jax.ShapeDtypeStruct((share, sets, lanes), f32)
    sizes = (cells_dev, sets, lanes, tile_slots, link_slots, row_bonds)
    chunks = 8
    return pl.pallas_call(
        functools.partial(kernel, rows, cols, sizes),
        out_shape=(out, out),
        in_specs=[smem] + [hbm] * 6 + [vmem] * 4,
        out_specs=(vmem, vmem),
        scratch_shapes=[
            pltpu.VMEM(hardness.shape, f32),
            pltpu.VMEM(bond_stiffness.shape, f32),
            pltpu.VMEM(link_ends.shape, i32),
            pltpu.VMEM(link_carry.shape, i32),
            pltpu.VMEM((tile_slots, lanes, lanes), f32),
            pltpu.VMEM((tile_slots, 2 * lanes, lanes), bf16),
            pltpu.VMEM((link_slots, lanes, lanes), bf16),
            pltpu.VMEM((link_slots, sets, lanes), f32),
            pltpu.VMEM((link_slots, sets, lanes), f32),
            pltpu.VMEM((link_slots, sets, lanes), f32),
            pltpu.VMEM((tile_slots, sets, lanes), f32),
            pltpu.VMEM((link_slots, sets, lanes), f32),
            pltpu.VMEM((rows, cells_dev, sets, lanes), f32),
            pltpu.VMEM((2, cols, block, lanes), f32),
            pltpu.VMEM((2, rows, block, lanes), f32),
            pltpu.VMEM((row_cells, 2 * sets, lanes), bf16),
            pltpu.VMEM((group_cells, 2 * sets, 2 * lanes), bf16),
            pltpu.VMEM((2, group_cells * sets, lanes), f32),
            pltpu.VMEM((2, rows, block, lanes), f32),
            pltpu.VMEM((2, row_cells * sets, lanes), f32),
            pltpu.VMEM((2, cols, block, lanes), f32),
            pltpu.VMEM((2, rows, block, lanes), f32),
            pltpu.VMEM((group_cells, 2 * sets, lanes), bf16),
            pltpu.VMEM((3, row_bonds * sets, lanes), f32),
            pltpu.VMEM((3, cols, share * sets, lanes), f32),
            pltpu.VMEM((2, rows, sets, lanes), f32),
            pltpu.VMEM((2, cols, sets, lanes), f32),
            pltpu.SemaphoreType.DMA((5,)),
            pltpu.SemaphoreType.DMA((chunks,)),
            pltpu.SemaphoreType.DMA((9, rows)),
            pltpu.SemaphoreType.DMA((9, rows)),
            pltpu.SemaphoreType.DMA((9, cols)),
            pltpu.SemaphoreType.DMA((9, cols)),
        ],
        compiler_params=pltpu.CompilerParams(
            collective_id=0, has_side_effects=True, vmem_limit_bytes=67043328
        ),
    )(
        table, charge_drive, hardness, bond_stiffness, coulomb_tiles, link_ends, link_carry,
        square, charge0, fixed, sums0,
    )


def solution(mesh):
    return jax.shard_map(
        on_device,
        mesh=mesh,
        in_specs=(
            P(("row", "col"), None, None),
            P(("row", "col"), None),
            P("row", None),
            P(("row", "col"), None, None),
            P(("row", "col")),
            P(("row", "col")),
            P(("row", "col")),
            P(("row", "col")),
            P(("row", "col")),
            P(("row", "col"), None, None),
            P(("row", "col"), None),
            P(("row", "col")),
        ),
        out_specs=(P(("row", "col"), None, None), P(("row", "col"), None, None)),
        check_vma=False,
    )
```

```python
import functools

import jax
import jax.numpy as jnp
from jax import lax
from jax.experimental import pallas as pl
from jax.experimental.pallas import tpu as pltpu
from jax.sharding import PartitionSpec as P

MESH = pl.DeviceIdType.MESH
NT = (((1,), (1,)), ((), ()))
NN = (((1,), (0,)), ((), ()))


def halves(value):
    high = value.astype(jnp.bfloat16)
    low = (value - high.astype(jnp.float32)).astype(jnp.bfloat16)
    return high, low


def dot(left, right, dims=NN):
    return lax.dot_general(left, right, dims, preferred_element_type=jnp.float32)


class Row:
    def __init__(self, rows, send, recv, started):
        self.rows, self.send, self.recv, self.started = rows, send, recv, started
        self.inner = 2 if rows % 2 == 0 else 1
        self.outer = rows // self.inner
        self.r, self.c = lax.axis_index("row"), lax.axis_index("col")
        self.high, self.low = self.r // self.inner, lax.rem(self.r, self.inner)

    def copy(self, phase, index, source, target, peer):
        copy = pltpu.make_async_remote_copy(
            src_ref=source, dst_ref=target,
            send_sem=self.send.at[phase, index], recv_sem=self.recv.at[phase, index],
            device_id=(peer, self.c), device_id_type=MESH,
        )
        copy.start()
        self.started.append(copy)
        return copy

    def partner(self, k):
        if self.outer & (self.outer - 1):
            half = self.outer + k
            return lax.rem(half - self.high, self.outer)
        place, bit = self.high, 1
        while bit < self.outer:
            if k & bit:
                place = place + bit - 2 * bit * lax.rem(self.high // bit, 2)
            bit *= 2
        return place

    def near_peer(self):
        return self.high * self.inner + self.inner - 1 - self.low

    def gather_begin(self, phase, source, slot_of):
        far = [
            self.copy(phase, k * self.inner, source, slot_of(self.r), self.partner(k) * self.inner + self.low)
            for k in range(1, self.outer)
        ]
        near = [
            self.copy(phase, 1, source, slot_of(self.r), self.near_peer())
            for _ in range(self.inner - 1)
        ]
        return far, near

    def gather_relay(self, phase, copies, slot_of, start=1, stop=None):
        far, near = copies
        for k in range(start, stop or self.outer):
            far[k - 1].wait_recv()
            if self.inner > 1:
                block = slot_of(self.partner(k) * self.inner + self.low)
                near.append(self.copy(phase, k * self.inner + 1, block, block, self.near_peer()))

    def gather_end(self, copies):
        for copy in copies[1]:
            copy.wait_recv()


def greet(rows, cols, r, c, with_cols):
    barrier = pltpu.get_barrier_semaphore()
    for k in range(1, rows):
        pl.semaphore_signal(barrier, inc=1, device_id=(lax.rem(r + k, rows), c), device_id_type=MESH)
    if with_cols:
        for k in range(1, cols):
            pl.semaphore_signal(barrier, inc=1, device_id=(r, lax.rem(c + k, cols)), device_id_type=MESH)
    return barrier


def link_kernel(
    rows, cols, sizes,
    tile_rows, tile_cols, link_bonds, link_cells, tiles_live, links_live, bonds, ends_hbm, carry, stiffness, tiles_hbm,
    table, ends_all, weight_all, cells_all, tile_parts, tile_turned,
    tiles, ids, sem, tile_sem, row_send, row_recv,
):
    link_slots, lanes = carry.shape
    width = ids.shape[1]
    started = []
    row = Row(rows, row_send, row_recv, started)
    r, c = row.r, row.c
    barrier = greet(rows, cols, r, c, False)
    own_ends = pltpu.make_async_copy(ends_hbm, ends_all.at[r], sem.at[2])
    own_ends.start()
    chunks = tile_sem.shape[0]
    per_chunk = tiles.shape[0] // chunks
    ids[...] = jnp.zeros_like(ids)
    copies = []
    for i, (source, target) in enumerate((
        (tile_rows, ids.at[0:1, 0 : tile_rows.shape[1]]), (tile_cols, ids.at[1:2, 0 : tile_cols.shape[1]]),
    )):
        copy = pltpu.make_async_copy(source, target, sem.at[i])
        copy.start()
        copies.append(copy)
    ids[2:3, 0:link_slots] = link_bonds[...]
    ids[3:4, 0:link_slots] = link_cells[...]
    tile_count, link_count = tiles_live[0], links_live[0]
    slot = lax.broadcasted_iota(jnp.int32, (1, width), 1)
    cells_all[r] = jnp.where(slot < link_count, ids[3:4, :], -1)
    for s in range(link_slots):
        live = jnp.full((1, lanes), s, jnp.int32) < link_count
        kept = jnp.where(live, carry[s : s + 1, :], 0).astype(jnp.float32)
        weight_all[r, s : s + 1, :] = kept * stiffness[pl.ds(bonds[0, s], 1), :]
    slots = (lambda i: ends_all.at[i]), (lambda i: weight_all.at[i]), (lambda i: cells_all.at[i])
    pl.semaphore_wait(barrier, rows - 1)
    gathers = [
        row.gather_begin(phase, ends_hbm if phase == 0 else of(r), of) for phase, of in enumerate(slots)
    ]
    tile_copies = []
    for i in range(chunks):
        part = pl.ds(i * per_chunk, per_chunk)
        copy = pltpu.make_async_copy(tiles_hbm.at[part], tiles.at[part], tile_sem.at[i])
        copy.start()
        tile_copies.append(copy)
    for copy in copies:
        copy.wait()
    beyond = 1 << 20
    down = lax.broadcasted_iota(jnp.int32, (width, width), 0)
    across = lax.broadcasted_iota(jnp.int32, (width, width), 1)

    def total(value, axis):
        return jnp.sum(value, axis=axis, keepdims=True)

    def column(value):
        return total(jnp.where(down == across, value, 0), 1)

    for place, (key_row, other, count) in enumerate((
        (0, 1, tile_count), (1, 0, tile_count), (3, 3, link_count), (2, 2, link_count),
    )):
        key = jnp.where(across[0:1] < count, ids[key_row : key_row + 1, :], beyond)
        mine = column(key)
        equal_before = total(jnp.where((key == mine) & (across < down), 1, 0), 1)
        rank = total(jnp.where(key < mine, 1, 0), 1) + equal_before
        here = rank == across
        upto = total(jnp.where(mine <= across, 1, 0), 0)
        fewer = total(jnp.where(mine < across, 1, 0), 0)
        at = 5 * place
        table[at : at + 1, :] = total(jnp.where(here, down, 0), 0)
        table[at + 1 : at + 2, :] = total(jnp.where(here & (equal_before > 0), 1, 0), 0)
        table[at + 2 : at + 3, :] = jnp.maximum(upto - 1, 0)
        table[at + 3 : at + 4, :] = jnp.where(upto > fewer, 1, 0)
        table[at + 4 : at + 5, :] = total(jnp.where(here, column(ids[other : other + 1, :]), 0), 0)
    table[20:22, :] = ids[2:4, :]
    table[22:24, :] = jnp.full((2, width), link_count, jnp.int32)

    identity = jnp.where(
        lax.broadcasted_iota(jnp.int32, (lanes, lanes), 0) == lax.broadcasted_iota(jnp.int32, (lanes, lanes), 1), 1.0, 0.0
    ).astype(jnp.bfloat16)

    def split_tiles(t, _):
        high, low = halves(tiles[t])
        tile_parts[t, 0:lanes, :] = high
        tile_parts[t, lanes : 2 * lanes, :] = low
        turned = dot(identity, jnp.concatenate([high, low], axis=0), NT)
        tile_turned[t] = turned.astype(jnp.bfloat16)
        return 0

    def split_chunks(start, stop):
        for i in range(start, stop):
            tile_copies[i].wait()

            def several(g, _):
                for e in range(8):
                    split_tiles(g * 8 + e, 0)
                return 0

            lax.fori_loop(i * per_chunk // 8, (i + 1) * per_chunk // 8, several, 0)

    split_chunks(0, chunks // 2)
    own_ends.wait()
    for phase, of in enumerate(slots):
        row.gather_relay(phase, gathers[phase], of)
    split_chunks(chunks // 2, chunks)
    for gather in gathers:
        row.gather_end(gather)
    for copy in started:
        copy.wait_send()


GROUP = 4


def cell_kernel(
    rows, sizes, cells, ends_all, weight_all, drive, square_out, charge_out, fixed_out, sums_out, listed, acc,
):
    cells_dev, sets, lanes, link_slots = sizes
    first = lax.axis_index("row") * cells_dev
    acc[...] = jnp.zeros_like(acc)

    def collect(i, found):
        for s in range(link_slots):
            local = cells[i, 0, s] - first
            listed[found] = (i * link_slots + s) * cells_dev + local
            found = found + jnp.where((local >= 0) & (local < cells_dev), 1, 0)
        return found

    found = lax.fori_loop(0, rows, collect, jnp.int32(0))
    for e in range(GROUP):
        listed[found + e] = 0
    atom = lax.broadcasted_iota(jnp.int32, (lanes, lanes), 0)

    def visit(g, sums):
        norm, energy = sums
        for e in range(GROUP):
            i = g * GROUP + e
            code = listed[i]
            s, l = code // cells_dev, lax.rem(code, cells_dev)
            real = jnp.full((1, lanes), i, jnp.int32) < found
            pair = ends_all[s]
            weight = jnp.where(real, weight_all[pl.ds(s, 1), :], 0.0)
            kept = jnp.where(weight != 0.0, 1.0, 0.0)
            gain = jnp.where(atom == pair[0:1, :], kept, 0.0)
            lose = jnp.where(atom == pair[1:2, :], kept, 0.0)
            matrix = (gain - lose).astype(jnp.bfloat16)
            high, low = halves(drive[l])
            both = dot(jnp.concatenate([high, low], axis=0), matrix)
            u = -(both[0:sets] + both[sets : 2 * sets])
            ku = weight * u
            norm = norm + u * u
            energy = energy + ku * u
            left = jnp.concatenate([matrix, *halves(u), *halves(ku)], axis=0)
            acc[l] += dot(left, matrix, NT)
        return norm, energy

    zero = jnp.zeros((sets, lanes), jnp.float32)
    norm, energy = lax.fori_loop(0, (found + GROUP - 1) // GROUP, visit, (zero, zero))
    sums_out[0] = norm
    sums_out[1] = energy
    for l in range(cells_dev):
        high, low = halves(acc[l, 0:lanes, :])
        square_out[l, :, 0:lanes] = high
        square_out[l, :, lanes : 2 * lanes] = low
        at = lanes
        charge_out[l] = acc[l, at : at + sets, :] + acc[l, at + sets : at + 2 * sets, :]
        at = lanes + 2 * sets
        fixed_out[l] = acc[l, at : at + sets, :] + acc[l, at + sets : at + 2 * sets, :]


def kernel(
    rows, cols, sizes,
    table, drive, hardness_hbm, stiffness_hbm, tile_parts, tile_turned, ends_hbm, carry_hbm, square, charge0, fixed, sums0,
    out_solution, out_residual,
    hardness, stiffness, ends, carry,
    incidence, u0, u1, u2, products, bond_products,
    drive_all, row_charge, col_charge,
    row_parts, col_parts, pot_part, pot_in, mirror_part, mirror_in, pot_all, pot_parts,
    bond_part, bond_in, dots_row, dots_col,
    small_sem, row_send, row_recv, col_send, col_recv,
):
    cells_dev, sets, lanes, tile_slots, link_slots, row_bonds = sizes
    group_cells, row_cells = rows * cells_dev, cols * cells_dev
    share = row_bonds // cols
    block = cells_dev * sets
    started = []
    row = Row(rows, row_send, row_recv, started)
    r, c = row.r, row.c

    small = []
    for i, (source, target) in enumerate((
        (ends_hbm, ends), (carry_hbm, carry),
        (hardness_hbm, hardness), (stiffness_hbm, stiffness), (drive, drive_all.at[r]),
    )):
        copy = pltpu.make_async_copy(source, target, small_sem.at[i])
        copy.start()
        small.append(copy)
    barrier = greet(rows, cols, r, c, True)
    for l in range(cells_dev):
        part = slice(l * sets, (l + 1) * sets)
        col_charge[0, r, part, :] = charge0[l]
        row_charge[0, c, part, :] = charge0[l]
    pl.semaphore_wait(barrier, rows + cols - 2)

    def send_row(phase, source, target):
        return [
            row.copy(phase, k, source(lax.rem(r + k, rows)), target, lax.rem(r + k, rows))
            for k in range(1, rows)
        ]

    def send_col(phase, source, target):
        copies = []
        for k in range(1, cols):
            peer = lax.rem(c + k, cols)
            copy = pltpu.make_async_remote_copy(
                src_ref=source(peer), dst_ref=target,
                send_sem=col_send.at[phase, k], recv_sem=col_recv.at[phase, k],
                device_id=(r, peer), device_id_type=MESH,
            )
            copy.start()
            copies.append(copy)
        started.extend(copies)
        return copies

    def arrive(copies):
        for copy in copies:
            copy.wait_recv()

    UNROLL = 32

    def slot(s):
        return pl.ds(pl.multiple_of(s * sets, sets), sets)

    def add_slots(place, value, running, carried, start, stop):
        def body(i, carried):
            for j in range(UNROLL):
                k = i * UNROLL + j
                kept = jnp.full((sets, lanes), table[5 * place + 1, k], jnp.int32).astype(jnp.float32)
                carried = carried * kept + value(k, table[5 * place, k], table[5 * place + 4, k])
                running[k] = carried
            return carried

        return lax.fori_loop(start // UNROLL, stop // UNROLL, body, carried)

    def spread_slots(place, size, running, target):
        def spread(i, _):
            for j in range(4):
                l = i * 4 + j
                some = jnp.full((sets, lanes), table[5 * place + 3, l], jnp.int32).astype(jnp.float32)
                found = running[table[5 * place + 2, l]]
                target[slot(l), :] = found * some
            return 0

        lax.fori_loop(0, size // 4, spread, 0)

    nothing = jnp.zeros((sets, lanes), jnp.float32)

    def to_bonds(potential_of, update):
        def fill(l, _):
            high, low = halves(potential_of(l))
            pot_parts[l, 0:sets, :] = high
            pot_parts[l, sets : 2 * sets, :] = low
            return 0

        lax.fori_loop(0, group_cells, fill, 0)

        def body(i, _):
            for j in range(UNROLL):
                s = i * UNROLL + j
                both = dot(pot_parts[table[21, s]], incidence[s])
                update(s, both[0:sets] + both[sets : 2 * sets])
            return 0

        lax.fori_loop(0, link_slots // UNROLL, body, 0)

    def send_bonds(n, u):
        add_slots(3, lambda k, s, _: u[s], bond_products, nothing, 0, link_slots)
        spread_slots(3, row_bonds, bond_products, bond_part.at[n])
        size = share * sets
        copies = send_col(
            4 + n,
            lambda peer: bond_part.at[n, pl.ds(pl.multiple_of(peer * size, size), size)],
            bond_in.at[n, c],
        )
        bond_in[n, c] = bond_part[n, pl.ds(pl.multiple_of(c * size, size), size), :]
        return copies

    def row_block(peer):
        return pl.ds(pl.multiple_of(peer * block, block), block)

    def drive_slot(i):
        return drive_all.at[i]

    def operate(n, background, prepare, middle):
        def charge_slot(i):
            return col_charge.at[n, i]

        side = send_col(n, lambda peer: row_charge.at[n, c], row_charge.at[n, c])
        gather = row.gather_begin(3 * n, col_charge.at[n, r], charge_slot)
        prepare()
        arrive(side)
        row.gather_relay(3 * n, gather, charge_slot, 1, 2)
        for k in range(cols):
            for l in range(cells_dev):
                high, low = halves(row_charge[n, k, l * sets : (l + 1) * sets, :])
                row_parts[k * cells_dev + l, 0:sets, :] = high
                row_parts[k * cells_dev + l, sets : 2 * sets, :] = low

        def forward(k, t, cell):
            both = dot(row_parts[cell], tile_turned[t])
            return both[0:sets, 0:lanes] + (
                both[sets : 2 * sets, 0:lanes] + both[0:sets, lanes : 2 * lanes]
            )

        half = tile_slots // (2 * UNROLL) * UNROLL
        carried = add_slots(0, forward, products, nothing, 0, half)
        row.gather_relay(3 * n, gather, charge_slot, 2)
        copies, other_slot, phase = background()
        add_slots(0, forward, products, carried, half, tile_slots)
        spread_slots(0, group_cells, products, pot_part.at[n])
        parts = send_row(3 * n + 1, lambda peer: pot_part.at[n, row_block(peer)], pot_in.at[n, r])
        pot_in[n, r] = pot_part[n, row_block(r), :]
        row.gather_end(gather)
        for k in range(rows):
            for l in range(cells_dev):
                high, low = halves(col_charge[n, k, l * sets : (l + 1) * sets, :])
                place = k * cells_dev + l
                col_parts[place, 0:sets, 0:lanes] = high
                col_parts[place, 0:sets, lanes : 2 * lanes] = high
                col_parts[place, sets : 2 * sets, 0:lanes] = low
                col_parts[place, sets : 2 * sets, lanes : 2 * lanes] = jnp.zeros_like(low)

        def backward(k, t, cell):
            both = dot(col_parts[cell], tile_parts[t])
            return both[0:sets] + both[sets : 2 * sets]

        add_slots(1, backward, products, nothing, 0, tile_slots)
        spread_slots(1, row_cells, products, mirror_part.at[n])
        side = send_col(2 + n, lambda peer: mirror_part.at[n, row_block(peer)], mirror_in.at[n, c])
        mirror_in[n, c] = mirror_part[n, row_block(c), :]
        middle()
        row.gather_relay(phase, copies, other_slot)
        arrive(parts)
        total = pot_in[n, 0]
        for k in range(1, rows):
            total = total + pot_in[n, k]
        arrive(side)
        for k in range(cols):
            total = total + mirror_in[n, k]
        own = col_charge[n, r]
        for l in range(cells_dev):
            part = slice(l * sets, (l + 1) * sets)
            pot_all[n, r, part, :] = total[part] + hardness[l : l + 1, :] * own[part]
        return copies

    def pot_slot(n):
        return lambda i: pot_all.at[n, i]

    def potential(n):
        return lambda l: pot_all[
            n, l // cells_dev, pl.ds(pl.multiple_of(lax.rem(l, cells_dev) * sets, sets), sets), :
        ]

    def own_cells(n, l):
        part = slice(l * sets, (l + 1) * sets)
        return col_charge[n, r, part, :], pot_all[n, r, part, :]

    def packed(a, b):
        a = jnp.sum(a, axis=1, keepdims=True)
        b = jnp.sum(b, axis=1, keepdims=True)
        lane = lax.broadcasted_iota(jnp.int32, (sets, lanes), 1)
        return jnp.where(lane == 0, a, jnp.where(lane == 1, b, 0.0))

    def dots_begin(n, values):
        dots_row[n, r] = values
        return send_row(7 + n, lambda peer: dots_row.at[n, r], dots_row.at[n, r])

    def dots_middle(n, copies):
        arrive(copies)
        total = dots_row[n, 0]
        for k in range(1, rows):
            total = total + dots_row[n, k]
        dots_col[n, c] = total
        return send_col(7 + n, lambda peer: dots_col.at[n, c], dots_col.at[n, c])

    def dots_end(n, copies):
        arrive(copies)
        total = dots_col[n, 0]
        for k in range(1, cols):
            total = total + dots_col[n, k]
        return total[:, 0:1], total[:, 1:2]

    state = {}

    def drive_background():
        return row.gather_begin(2, drive, drive_slot), drive_slot, 2

    def finish_small():
        link_count = table[22, 0]
        small[0].wait()
        small[1].wait()

        def build_incidence(s, _):
            atom = lax.broadcasted_iota(jnp.int32, (lanes, lanes), 0)
            pair = ends[s]
            live = jnp.full((1, lanes), s, jnp.int32) < link_count
            kept = jnp.where(live, carry[pl.ds(s, 1), :], 0).astype(jnp.float32)
            gain = jnp.where(atom == pair[0:1, :], kept, 0.0)
            lose = jnp.where(atom == pair[1:2, :], kept, 0.0)
            incidence[s] = (gain - lose).astype(jnp.bfloat16)
            return 0

        lax.fori_loop(0, link_slots, build_incidence, 0)
        for copy in small[2:]:
            copy.wait()

    def first_bonds():
        row.gather_end(state["drive"])
        def first(s, value):
            u0[s] = -value

        to_bonds(lambda l: drive_all[l // cells_dev, lax.rem(l, cells_dev)], first)
        state["bonds0"] = send_bonds(0, u0)

    state["drive"] = operate(0, drive_background, finish_small, lambda: None)

    energy = sums0[1]
    for l in range(cells_dev):
        part = slice(l * sets, (l + 1) * sets)
        charge, value = own_cells(0, l)
        both = dot(jnp.concatenate(halves(value), axis=0), square[l])
        new = both[0:sets, 0:lanes] + (
            both[sets : 2 * sets, 0:lanes] + both[0:sets, lanes : 2 * lanes]
        )
        new = new + fixed[l]
        col_charge[1, r, part, :] = new
        row_charge[1, c, part, :] = new
        energy = energy + charge * value

    def potential_background():
        gather = row.gather_begin(5, pot_all.at[0, r], pot_slot(0))
        state["dots"] = dots_begin(0, packed(sums0[0], energy))
        return gather, pot_slot(0), 5

    def first_dots():
        state["dots"] = dots_middle(0, state["dots"])

    def second_bonds(copies):
        row.gather_end(copies)
        def update(s, value):
            u1[s] = value + stiffness[pl.ds(table[20, s], 1), :] * u0[s]

        to_bonds(potential(0), update)
        state["bonds1"] = send_bonds(1, u1)
        norm, energy = dots_end(0, state["dots"])
        state["norm"], state["step"] = norm, norm / energy

        def body(i, sums):
            a, b = sums
            for j in range(4):
                s = i * 4 + j
                residual = u0[s] - state["step"] * u1[s]
                square_of = residual * residual
                a = a + square_of
                b = b + stiffness[pl.ds(table[20, s], 1), :] * square_of
            return a, b

        state["sums"] = lax.fori_loop(0, link_slots // 4, body, (nothing, nothing))

    copies = operate(1, potential_background, first_bonds, first_dots)
    gather = row.gather_begin(6, pot_all.at[1, r], pot_slot(1))
    second_bonds(copies)
    norm0, step0 = state["norm"], state["step"]
    norm_part, energy_part = state["sums"]
    for l in range(cells_dev):
        charge, value = own_cells(0, l)
        charge1, value1 = own_cells(1, l)
        energy_part = energy_part + (charge - step0 * charge1) * (value - step0 * value1)
    copies = dots_begin(1, packed(norm_part, energy_part))
    row.gather_relay(6, gather, pot_slot(1))
    copies = dots_middle(1, copies)
    row.gather_end(gather)

    def last(s, value):
        u2[s] = value + stiffness[pl.ds(table[20, s], 1), :] * u1[s]

    to_bonds(potential(1), last)
    bonds2 = send_bonds(2, u2)
    norm1, energy1 = dots_end(1, copies)
    arrive(state["bonds0"])
    arrive(state["bonds1"])
    arrive(bonds2)
    gain = norm1 / norm0
    step1 = norm1 / (energy1 - gain * norm1 / step0)
    for j in range(share):
        part = slice(j * sets, (j + 1) * sets)
        total = []
        for n in range(3):
            value = bond_in[n, 0, part, :]
            for k in range(1, cols):
                value = value + bond_in[n, k, part, :]
            total.append(value)
        residual = total[0] - step0 * total[1]
        applied = total[1] - step0 * total[2]
        out_solution[j] = step0 * total[0] + step1 * (residual + gain * total[0])
        out_residual[j] = residual - step1 * (applied + gain * total[1])
    for copy in started:
        copy.wait_send()


def on_device(
    charge_drive,
    hardness,
    bond_stiffness,
    coulomb_tiles,
    tile_rows,
    tile_cols,
    tile_count,
    link_bonds,
    link_cells,
    link_ends,
    link_carry,
    link_count,
):
    rows, cols = lax.axis_size("row"), lax.axis_size("col")
    cells_dev, sets, lanes = charge_drive.shape
    tile_slots, link_slots = coulomb_tiles.shape[0], link_bonds.shape[0]
    row_bonds = bond_stiffness.shape[0]
    group_cells, row_cells = rows * cells_dev, cols * cells_dev
    share = row_bonds // cols
    block = cells_dev * sets
    f32, bf16, i32 = jnp.float32, jnp.bfloat16, jnp.int32
    vmem = pl.BlockSpec(memory_space=pltpu.VMEM)
    smem = pl.BlockSpec(memory_space=pltpu.SMEM)
    hbm = pl.BlockSpec(memory_space=pltpu.HBM)
    width = -(-max(tile_slots, link_slots, group_cells, row_bonds) // 128) * 128
    bonds = link_bonds.reshape(1, -1)
    coulomb_tiles, link_ends, link_carry, bond_stiffness, charge_drive, hardness, tile_rows, tile_cols, bonds, link_cells = (
        pltpu.with_memory_space_constraint(x, pltpu.HBM) for x in
        (coulomb_tiles, link_ends, link_carry, bond_stiffness, charge_drive, hardness,
         tile_rows.reshape(1, -1), tile_cols.reshape(1, -1), bonds, link_cells.reshape(1, -1))
    )
    chunks = 8
    table, ends_all, weight_all, cells_all, tile_parts, tile_turned = pl.pallas_call(
        functools.partial(link_kernel, rows, cols, None),
        out_shape=(
            jax.ShapeDtypeStruct((24, width), i32),
            jax.ShapeDtypeStruct((rows, *link_ends.shape), i32),
            jax.ShapeDtypeStruct((rows, link_slots, lanes), f32),
            jax.ShapeDtypeStruct((rows, 1, width), i32),
            jax.ShapeDtypeStruct((tile_slots, 2 * lanes, lanes), bf16),
            jax.ShapeDtypeStruct((tile_slots, lanes, 2 * lanes), bf16),
        ),
        in_specs=[hbm] * 2 + [vmem] * 2 + [smem] * 3 + [hbm] + [vmem] * 2 + [hbm],
        out_specs=(vmem,) * 6,
        scratch_shapes=[
            pltpu.VMEM((tile_slots, lanes, lanes), f32),
            pltpu.VMEM((8, width), i32),
            pltpu.SemaphoreType.DMA((3,)),
            pltpu.SemaphoreType.DMA((chunks,)),
            pltpu.SemaphoreType.DMA((3, rows)),
            pltpu.SemaphoreType.DMA((3, rows)),
        ],
        compiler_params=pltpu.CompilerParams(
            collective_id=1, has_side_effects=True, vmem_limit_bytes=32 << 20
        ),
    )(
        tile_rows, tile_cols, bonds, link_cells,
        tile_count, link_count, bonds, link_ends, link_carry, bond_stiffness, coulomb_tiles,
    )
    square, charge0, fixed, sums0 = pl.pallas_call(
        functools.partial(cell_kernel, rows, (cells_dev, sets, lanes, link_slots)),
        out_shape=(
            jax.ShapeDtypeStruct((cells_dev, lanes, 2 * lanes), bf16),
            jax.ShapeDtypeStruct((cells_dev, sets, lanes), f32),
            jax.ShapeDtypeStruct((cells_dev, sets, lanes), f32),
            jax.ShapeDtypeStruct((2, sets, lanes), f32),
        ),
        in_specs=[smem] + [vmem] * 3,
        out_specs=(vmem,) * 4,
        scratch_shapes=[
            pltpu.SMEM((rows * link_slots + 2 * GROUP,), i32),
            pltpu.VMEM((cells_dev, lanes + 4 * sets, lanes), f32),
        ],
        compiler_params=pltpu.CompilerParams(vmem_limit_bytes=16 << 20),
    )(
        cells_all, ends_all.reshape(rows * link_slots, *link_ends.shape[1:]),
        weight_all.reshape(rows * link_slots, lanes), charge_drive,
    )
    out = jax.ShapeDtypeStruct((share, sets, lanes), f32)
    sizes = (cells_dev, sets, lanes, tile_slots, link_slots, row_bonds)
    return pl.pallas_call(
        functools.partial(kernel, rows, cols, sizes),
        out_shape=(out, out),
        in_specs=[smem] + [hbm] * 3 + [vmem] * 2 + [hbm] * 2 + [vmem] * 4,
        out_specs=(vmem, vmem),
        scratch_shapes=[
            pltpu.VMEM(hardness.shape, f32),
            pltpu.VMEM(bond_stiffness.shape, f32),
            pltpu.VMEM(link_ends.shape, i32),
            pltpu.VMEM(link_carry.shape, i32),
            pltpu.VMEM((link_slots, lanes, lanes), bf16),
            pltpu.VMEM((link_slots, sets, lanes), f32),
            pltpu.VMEM((link_slots, sets, lanes), f32),
            pltpu.VMEM((link_slots, sets, lanes), f32),
            pltpu.VMEM((tile_slots, sets, lanes), f32),
            pltpu.VMEM((link_slots, sets, lanes), f32),
            pltpu.VMEM((rows, cells_dev, sets, lanes), f32),
            pltpu.VMEM((2, cols, block, lanes), f32),
            pltpu.VMEM((2, rows, block, lanes), f32),
            pltpu.VMEM((row_cells, 2 * sets, lanes), bf16),
            pltpu.VMEM((group_cells, 2 * sets, 2 * lanes), bf16),
            pltpu.VMEM((2, group_cells * sets, lanes), f32),
            pltpu.VMEM((2, rows, block, lanes), f32),
            pltpu.VMEM((2, row_cells * sets, lanes), f32),
            pltpu.VMEM((2, cols, block, lanes), f32),
            pltpu.VMEM((2, rows, block, lanes), f32),
            pltpu.VMEM((group_cells, 2 * sets, lanes), bf16),
            pltpu.VMEM((3, row_bonds * sets, lanes), f32),
            pltpu.VMEM((3, cols, share * sets, lanes), f32),
            pltpu.VMEM((2, rows, sets, lanes), f32),
            pltpu.VMEM((2, cols, sets, lanes), f32),
            pltpu.SemaphoreType.DMA((5,)),
            pltpu.SemaphoreType.DMA((9, rows)),
            pltpu.SemaphoreType.DMA((9, rows)),
            pltpu.SemaphoreType.DMA((9, cols)),
            pltpu.SemaphoreType.DMA((9, cols)),
        ],
        compiler_params=pltpu.CompilerParams(
            collective_id=0, has_side_effects=True, vmem_limit_bytes=32 << 20
        ),
    )(
        table, charge_drive, hardness, bond_stiffness, tile_parts, tile_turned, link_ends, link_carry,
        square, charge0, fixed, sums0,
    )


def solution(mesh):
    return jax.shard_map(
        on_device,
        mesh=mesh,
        in_specs=(
            P(("row", "col"), None, None),
            P(("row", "col"), None),
            P("row", None),
            P(("row", "col"), None, None),
            P(("row", "col")),
            P(("row", "col")),
            P(("row", "col")),
            P(("row", "col")),
            P(("row", "col")),
            P(("row", "col"), None, None),
            P(("row", "col"), None),
            P(("row", "col")),
        ),
        out_specs=(P(("row", "col"), None, None), P(("row", "col"), None, None)),
        check_vma=False,
    )
```

```python
import functools

import jax
import jax.numpy as jnp
from jax import lax
from jax.experimental import pallas as pl
from jax.experimental.pallas import tpu as pltpu
from jax.sharding import PartitionSpec as P

MESH = pl.DeviceIdType.MESH
NT = (((1,), (1,)), ((), ()))
NN = (((1,), (0,)), ((), ()))


def halves(value):
    high = value.astype(jnp.bfloat16)
    low = (value - high.astype(jnp.float32)).astype(jnp.bfloat16)
    return high, low


def dot(left, right, dims=NN):
    return lax.dot_general(left, right, dims, preferred_element_type=jnp.float32)


class Row:
    def __init__(self, rows, send, recv, started):
        self.rows, self.send, self.recv, self.started = rows, send, recv, started
        self.inner = 2 if rows % 2 == 0 else 1
        self.outer = rows // self.inner
        self.r, self.c = lax.axis_index("row"), lax.axis_index("col")
        self.high, self.low = self.r // self.inner, lax.rem(self.r, self.inner)

    def copy(self, phase, index, source, target, peer):
        copy = pltpu.make_async_remote_copy(
            src_ref=source, dst_ref=target,
            send_sem=self.send.at[phase, index], recv_sem=self.recv.at[phase, index],
            device_id=(peer, self.c), device_id_type=MESH,
        )
        copy.start()
        self.started.append(copy)
        return copy

    def partner(self, k):
        if self.outer & (self.outer - 1):
            half = self.outer + k
            return lax.rem(half - self.high, self.outer)
        place, bit = self.high, 1
        while bit < self.outer:
            if k & bit:
                place = place + bit - 2 * bit * lax.rem(self.high // bit, 2)
            bit *= 2
        return place

    def near_peer(self):
        return self.high * self.inner + self.inner - 1 - self.low

    def gather_begin(self, phase, source, slot_of):
        far = [
            self.copy(phase, k * self.inner, source, slot_of(self.r), self.partner(k) * self.inner + self.low)
            for k in range(1, self.outer)
        ]
        near = [
            self.copy(phase, 1, source, slot_of(self.r), self.near_peer())
            for _ in range(self.inner - 1)
        ]
        return far, near

    def gather_relay(self, phase, copies, slot_of, start=1, stop=None):
        far, near = copies
        for k in range(start, stop or self.outer):
            far[k - 1].wait_recv()
            if self.inner > 1:
                block = slot_of(self.partner(k) * self.inner + self.low)
                near.append(self.copy(phase, k * self.inner + 1, block, block, self.near_peer()))

    def gather_end(self, copies):
        for copy in copies[1]:
            copy.wait_recv()


def greet(rows, cols, r, c, with_cols):
    barrier = pltpu.get_barrier_semaphore()
    for k in range(1, rows):
        pl.semaphore_signal(barrier, inc=1, device_id=(lax.rem(r + k, rows), c), device_id_type=MESH)
    if with_cols:
        for k in range(1, cols):
            pl.semaphore_signal(barrier, inc=1, device_id=(r, lax.rem(c + k, cols)), device_id_type=MESH)
    return barrier


def link_kernel(
    rows, cols, sizes,
    tile_rows, tile_cols, link_bonds, link_cells, tiles_live, links_live, bonds, ends_hbm, carry, stiffness, tiles_hbm,
    table, ends_all, weight_all, cells_all, tile_parts, tile_turned,
    tiles, ids, sem, tile_sem, row_send, row_recv,
):
    link_slots, lanes = carry.shape
    width = ids.shape[1]
    started = []
    row = Row(rows, row_send, row_recv, started)
    r, c = row.r, row.c
    barrier = greet(rows, cols, r, c, False)
    own_ends = pltpu.make_async_copy(ends_hbm, ends_all.at[r], sem.at[2])
    own_ends.start()
    chunks = tile_sem.shape[0]
    per_chunk = tiles.shape[0] // chunks
    ids[...] = jnp.zeros_like(ids)
    copies = []
    for i, (source, target) in enumerate((
        (tile_rows, ids.at[0:1, 0 : tile_rows.shape[1]]), (tile_cols, ids.at[1:2, 0 : tile_cols.shape[1]]),
    )):
        copy = pltpu.make_async_copy(source, target, sem.at[i])
        copy.start()
        copies.append(copy)
    ids[2:3, 0:link_slots] = link_bonds[...]
    ids[3:4, 0:link_slots] = link_cells[...]
    tile_count, link_count = tiles_live[0], links_live[0]
    slot = lax.broadcasted_iota(jnp.int32, (1, width), 1)
    cells_all[r] = jnp.where(slot < link_count, ids[3:4, :], -1)
    for s in range(link_slots):
        live = jnp.full((1, lanes), s, jnp.int32) < link_count
        kept = jnp.where(live, carry[s : s + 1, :], 0).astype(jnp.float32)
        weight_all[r, s : s + 1, :] = kept * stiffness[pl.ds(bonds[0, s], 1), :]
    slots = (lambda i: ends_all.at[i]), (lambda i: weight_all.at[i]), (lambda i: cells_all.at[i])
    pl.semaphore_wait(barrier, rows - 1)
    gathers = [
        row.gather_begin(phase, ends_hbm if phase == 0 else of(r), of) for phase, of in enumerate(slots)
    ]
    tile_copies = []
    for i in range(chunks):
        part = pl.ds(i * per_chunk, per_chunk)
        copy = pltpu.make_async_copy(tiles_hbm.at[part], tiles.at[part], tile_sem.at[i])
        copy.start()
        tile_copies.append(copy)
    for copy in copies:
        copy.wait()
    beyond = 1 << 20
    down = lax.broadcasted_iota(jnp.int32, (width, width), 0)
    across = lax.broadcasted_iota(jnp.int32, (width, width), 1)

    def total(value, axis):
        return jnp.sum(value, axis=axis, keepdims=True)

    def column(value):
        return total(jnp.where(down == across, value, 0), 1)

    for place, (key_row, other, count) in enumerate((
        (0, 1, tile_count), (1, 0, tile_count), (3, 3, link_count), (2, 2, link_count),
    )):
        key = jnp.where(across[0:1] < count, ids[key_row : key_row + 1, :], beyond)
        mine = column(key)
        equal_before = total(jnp.where((key == mine) & (across < down), 1, 0), 1)
        rank = total(jnp.where(key < mine, 1, 0), 1) + equal_before
        here = rank == across
        upto = total(jnp.where(mine <= across, 1, 0), 0)
        fewer = total(jnp.where(mine < across, 1, 0), 0)
        at = 5 * place
        table[at : at + 1, :] = total(jnp.where(here, down, 0), 0)
        table[at + 1 : at + 2, :] = total(jnp.where(here & (equal_before > 0), 1, 0), 0)
        table[at + 2 : at + 3, :] = jnp.maximum(upto - 1, 0)
        table[at + 3 : at + 4, :] = jnp.where(upto > fewer, 1, 0)
        table[at + 4 : at + 5, :] = total(jnp.where(here, column(ids[other : other + 1, :]), 0), 0)
    table[20:22, :] = ids[2:4, :]
    table[22:24, :] = jnp.full((2, width), link_count, jnp.int32)

    identity = jnp.where(
        lax.broadcasted_iota(jnp.int32, (lanes, lanes), 0) == lax.broadcasted_iota(jnp.int32, (lanes, lanes), 1), 1.0, 0.0
    ).astype(jnp.bfloat16)

    def split_tiles(t, _):
        high, low = halves(tiles[t])
        tile_parts[t, 0:lanes, :] = high
        tile_parts[t, lanes : 2 * lanes, :] = low
        turned = dot(identity, jnp.concatenate([high, low], axis=0), NT)
        tile_turned[t] = turned.astype(jnp.bfloat16)
        return 0

    def split_chunks(start, stop):
        for i in range(start, stop):
            tile_copies[i].wait()

            def several(g, _):
                for e in range(8):
                    split_tiles(g * 8 + e, 0)
                return 0

            lax.fori_loop(i * per_chunk // 8, (i + 1) * per_chunk // 8, several, 0)

    split_chunks(0, chunks * 5 // 8)
    own_ends.wait()
    for phase, of in enumerate(slots):
        row.gather_relay(phase, gathers[phase], of)
    split_chunks(chunks * 5 // 8, chunks)
    for gather in gathers:
        row.gather_end(gather)
    for copy in started:
        copy.wait_send()


GROUP = 8


def cell_kernel(
    rows, sizes, cells, ends_all, weight_all, drive, square_out, charge_out, fixed_out, sums_out, listed, acc,
):
    cells_dev, sets, lanes, link_slots = sizes
    first = lax.axis_index("row") * cells_dev
    acc[...] = jnp.zeros_like(acc)

    def collect(i, found):
        for s in range(link_slots):
            local = cells[i, 0, s] - first
            listed[found] = (i * link_slots + s) * cells_dev + local
            found = found + jnp.where((local >= 0) & (local < cells_dev), 1, 0)
        return found

    found = lax.fori_loop(0, rows, collect, jnp.int32(0))
    for e in range(GROUP):
        listed[found + e] = 0
    atom = lax.broadcasted_iota(jnp.int32, (lanes, lanes), 0)

    def visit(g, sums):
        norm, energy = sums
        for e in range(GROUP):
            i = g * GROUP + e
            code = listed[i]
            s, l = code // cells_dev, lax.rem(code, cells_dev)
            real = jnp.full((1, lanes), i, jnp.int32) < found
            pair = ends_all[s]
            weight = jnp.where(real, weight_all[pl.ds(s, 1), :], 0.0)
            kept = jnp.where(weight != 0.0, 1.0, 0.0)
            gain = jnp.where(atom == pair[0:1, :], kept, 0.0)
            lose = jnp.where(atom == pair[1:2, :], kept, 0.0)
            matrix = (gain - lose).astype(jnp.bfloat16)
            high, low = halves(drive[l])
            both = dot(jnp.concatenate([high, low], axis=0), matrix)
            u = -(both[0:sets] + both[sets : 2 * sets])
            ku = weight * u
            norm = norm + u * u
            energy = energy + ku * u
            left = jnp.concatenate([matrix, *halves(u), *halves(ku)], axis=0)
            acc[l] += dot(left, matrix, NT)
        return norm, energy

    zero = jnp.zeros((sets, lanes), jnp.float32)
    norm, energy = lax.fori_loop(0, (found + GROUP - 1) // GROUP, visit, (zero, zero))
    sums_out[0] = norm
    sums_out[1] = energy
    for l in range(cells_dev):
        high, low = halves(acc[l, 0:lanes, :])
        square_out[l, :, 0:lanes] = high
        square_out[l, :, lanes : 2 * lanes] = low
        at = lanes
        charge_out[l] = acc[l, at : at + sets, :] + acc[l, at + sets : at + 2 * sets, :]
        at = lanes + 2 * sets
        fixed_out[l] = acc[l, at : at + sets, :] + acc[l, at + sets : at + 2 * sets, :]


def kernel(
    rows, cols, sizes,
    table, drive, hardness_hbm, stiffness_hbm, tile_parts, tile_turned, ends_hbm, carry_hbm, square, charge0, fixed, sums0,
    out_solution, out_residual,
    hardness, stiffness, ends, carry,
    incidence, u0, u1, u2, products, bond_products,
    drive_all, row_charge, col_charge,
    row_parts, col_parts, pot_part, pot_in, mirror_part, mirror_in, pot_all, pot_parts,
    bond_part, bond_in, dots_row, dots_col,
    small_sem, row_send, row_recv, col_send, col_recv,
):
    cells_dev, sets, lanes, tile_slots, link_slots, row_bonds = sizes
    group_cells, row_cells = rows * cells_dev, cols * cells_dev
    share = row_bonds // cols
    block = cells_dev * sets
    started = []
    row = Row(rows, row_send, row_recv, started)
    r, c = row.r, row.c

    small = []
    for i, (source, target) in enumerate((
        (ends_hbm, ends), (carry_hbm, carry),
        (hardness_hbm, hardness), (stiffness_hbm, stiffness), (drive, drive_all.at[r]),
    )):
        copy = pltpu.make_async_copy(source, target, small_sem.at[i])
        copy.start()
        small.append(copy)
    barrier = greet(rows, cols, r, c, True)
    for l in range(cells_dev):
        part = slice(l * sets, (l + 1) * sets)
        col_charge[0, r, part, :] = charge0[l]
        row_charge[0, c, part, :] = charge0[l]
    pl.semaphore_wait(barrier, rows + cols - 2)

    def send_row(phase, source, target):
        copies = []
        for k in range(rows - 1, 0, -1):
            peer = row.partner(k // row.inner) * row.inner + lax.rem(row.low + k % row.inner, row.inner)
            copies.append(row.copy(phase, k, source(peer), target, peer))
        return copies

    def send_col(phase, source, target):
        copies = []
        for k in range(1, cols):
            peer = lax.rem(c + k, cols)
            copy = pltpu.make_async_remote_copy(
                src_ref=source(peer), dst_ref=target,
                send_sem=col_send.at[phase, k], recv_sem=col_recv.at[phase, k],
                device_id=(r, peer), device_id_type=MESH,
            )
            copy.start()
            copies.append(copy)
        started.extend(copies)
        return copies

    def arrive(copies):
        for copy in copies:
            copy.wait_recv()

    UNROLL = 32

    def slot(s):
        return pl.ds(pl.multiple_of(s * sets, sets), sets)

    def add_slots(place, value, running, carried, start, stop):
        def body(i, carried):
            for j in range(UNROLL):
                k = i * UNROLL + j
                kept = jnp.full((sets, lanes), table[5 * place + 1, k], jnp.int32).astype(jnp.float32)
                carried = carried * kept + value(k, table[5 * place, k], table[5 * place + 4, k])
                running[k] = carried
            return carried

        return lax.fori_loop(start // UNROLL, stop // UNROLL, body, carried)

    def spread_slots(place, size, running, target):
        def spread(i, _):
            for j in range(4):
                l = i * 4 + j
                some = jnp.full((sets, lanes), table[5 * place + 3, l], jnp.int32).astype(jnp.float32)
                found = running[table[5 * place + 2, l]]
                target[slot(l), :] = found * some
            return 0

        lax.fori_loop(0, size // 4, spread, 0)

    nothing = jnp.zeros((sets, lanes), jnp.float32)

    def to_bonds(potential_of, update):
        def fill(l, _):
            high, low = halves(potential_of(l))
            pot_parts[l, 0:sets, :] = high
            pot_parts[l, sets : 2 * sets, :] = low
            return 0

        lax.fori_loop(0, group_cells, fill, 0)

        def body(i, _):
            for j in range(UNROLL):
                s = i * UNROLL + j
                both = dot(pot_parts[table[21, s]], incidence[s])
                update(s, both[0:sets] + both[sets : 2 * sets])
            return 0

        lax.fori_loop(0, link_slots // UNROLL, body, 0)

    def send_bonds(n, u):
        add_slots(3, lambda k, s, _: u[s], bond_products, nothing, 0, link_slots)
        spread_slots(3, row_bonds, bond_products, bond_part.at[n])
        size = share * sets
        copies = send_col(
            4 + n,
            lambda peer: bond_part.at[n, pl.ds(pl.multiple_of(peer * size, size), size)],
            bond_in.at[n, c],
        )
        bond_in[n, c] = bond_part[n, pl.ds(pl.multiple_of(c * size, size), size), :]
        return copies

    def row_block(peer):
        return pl.ds(pl.multiple_of(peer * block, block), block)

    def drive_slot(i):
        return drive_all.at[i]

    def operate(n, background, prepare, middle):
        def charge_slot(i):
            return col_charge.at[n, i]

        side = send_col(n, lambda peer: row_charge.at[n, c], row_charge.at[n, c])
        gather = row.gather_begin(3 * n, col_charge.at[n, r], charge_slot)
        copies, other_slot, phase = background()
        prepare()
        arrive(side)
        row.gather_relay(3 * n, gather, charge_slot, 1, 2)
        for k in range(cols):
            for l in range(cells_dev):
                high, low = halves(row_charge[n, k, l * sets : (l + 1) * sets, :])
                row_parts[k * cells_dev + l, 0:sets, :] = high
                row_parts[k * cells_dev + l, sets : 2 * sets, :] = low

        def forward(k, t, cell):
            both = dot(row_parts[cell], tile_turned[t])
            return both[0:sets, 0:lanes] + (
                both[sets : 2 * sets, 0:lanes] + both[0:sets, lanes : 2 * lanes]
            )

        half = tile_slots // (2 * UNROLL) * UNROLL
        carried = add_slots(0, forward, products, nothing, 0, half)
        row.gather_relay(3 * n, gather, charge_slot, 2)
        add_slots(0, forward, products, carried, half, tile_slots)
        spread_slots(0, group_cells, products, pot_part.at[n])
        parts = send_row(3 * n + 1, lambda peer: pot_part.at[n, row_block(peer)], pot_in.at[n, r])
        pot_in[n, r] = pot_part[n, row_block(r), :]
        row.gather_end(gather)
        for k in range(rows):
            for l in range(cells_dev):
                high, low = halves(col_charge[n, k, l * sets : (l + 1) * sets, :])
                place = k * cells_dev + l
                col_parts[place, 0:sets, 0:lanes] = high
                col_parts[place, 0:sets, lanes : 2 * lanes] = high
                col_parts[place, sets : 2 * sets, 0:lanes] = low
                col_parts[place, sets : 2 * sets, lanes : 2 * lanes] = jnp.zeros_like(low)

        def backward(k, t, cell):
            both = dot(col_parts[cell], tile_parts[t])
            return both[0:sets] + both[sets : 2 * sets]

        add_slots(1, backward, products, nothing, 0, tile_slots)
        spread_slots(1, row_cells, products, mirror_part.at[n])
        side = send_col(2 + n, lambda peer: mirror_part.at[n, row_block(peer)], mirror_in.at[n, c])
        mirror_in[n, c] = mirror_part[n, row_block(c), :]
        row.gather_relay(phase, copies, other_slot)
        middle()
        arrive(parts)
        total = pot_in[n, 0]
        for k in range(1, rows):
            total = total + pot_in[n, k]
        arrive(side)
        for k in range(cols):
            total = total + mirror_in[n, k]
        own = col_charge[n, r]
        for l in range(cells_dev):
            part = slice(l * sets, (l + 1) * sets)
            pot_all[n, r, part, :] = total[part] + hardness[l : l + 1, :] * own[part]
        return copies

    def pot_slot(n):
        return lambda i: pot_all.at[n, i]

    def potential(n):
        return lambda l: pot_all[
            n, l // cells_dev, pl.ds(pl.multiple_of(lax.rem(l, cells_dev) * sets, sets), sets), :
        ]

    def own_cells(n, l):
        part = slice(l * sets, (l + 1) * sets)
        return col_charge[n, r, part, :], pot_all[n, r, part, :]

    def packed(a, b):
        a = jnp.sum(a, axis=1, keepdims=True)
        b = jnp.sum(b, axis=1, keepdims=True)
        lane = lax.broadcasted_iota(jnp.int32, (sets, lanes), 1)
        return jnp.where(lane == 0, a, jnp.where(lane == 1, b, 0.0))

    def dots_begin(n, values):
        dots_row[n, r] = values
        return send_row(7 + n, lambda peer: dots_row.at[n, r], dots_row.at[n, r])

    def dots_middle(n, copies):
        arrive(copies)
        total = dots_row[n, 0]
        for k in range(1, rows):
            total = total + dots_row[n, k]
        dots_col[n, c] = total
        return send_col(7 + n, lambda peer: dots_col.at[n, c], dots_col.at[n, c])

    def dots_end(n, copies):
        arrive(copies)
        total = dots_col[n, 0]
        for k in range(1, cols):
            total = total + dots_col[n, k]
        return total[:, 0:1], total[:, 1:2]

    state = {}

    def drive_background():
        return row.gather_begin(2, drive, drive_slot), drive_slot, 2

    def finish_small():
        link_count = table[22, 0]
        small[0].wait()
        small[1].wait()

        def build_incidence(s, _):
            atom = lax.broadcasted_iota(jnp.int32, (lanes, lanes), 0)
            pair = ends[s]
            live = jnp.full((1, lanes), s, jnp.int32) < link_count
            kept = jnp.where(live, carry[pl.ds(s, 1), :], 0).astype(jnp.float32)
            gain = jnp.where(atom == pair[0:1, :], kept, 0.0)
            lose = jnp.where(atom == pair[1:2, :], kept, 0.0)
            incidence[s] = (gain - lose).astype(jnp.bfloat16)
            return 0

        lax.fori_loop(0, link_slots, build_incidence, 0)
        for copy in small[2:]:
            copy.wait()

    def first_bonds():
        row.gather_end(state["drive"])
        def first(s, value):
            u0[s] = -value

        to_bonds(lambda l: drive_all[l // cells_dev, lax.rem(l, cells_dev)], first)
        state["bonds0"] = send_bonds(0, u0)

    state["drive"] = operate(0, drive_background, finish_small, lambda: None)

    energy = sums0[1]
    for l in range(cells_dev):
        part = slice(l * sets, (l + 1) * sets)
        charge, value = own_cells(0, l)
        both = dot(jnp.concatenate(halves(value), axis=0), square[l])
        new = both[0:sets, 0:lanes] + (
            both[sets : 2 * sets, 0:lanes] + both[0:sets, lanes : 2 * lanes]
        )
        new = new + fixed[l]
        col_charge[1, r, part, :] = new
        row_charge[1, c, part, :] = new
        energy = energy + charge * value

    def potential_background():
        gather = row.gather_begin(5, pot_all.at[0, r], pot_slot(0))
        state["dots"] = dots_begin(0, packed(sums0[0], energy))
        return gather, pot_slot(0), 5

    def first_dots():
        state["dots"] = dots_middle(0, state["dots"])

    def second_bonds(copies):
        row.gather_end(copies)
        def update(s, value):
            u1[s] = value + stiffness[pl.ds(table[20, s], 1), :] * u0[s]

        to_bonds(potential(0), update)
        state["bonds1"] = send_bonds(1, u1)
        norm, energy = dots_end(0, state["dots"])
        state["norm"], state["step"] = norm, norm / energy

        def body(i, sums):
            a, b = sums
            for j in range(4):
                s = i * 4 + j
                residual = u0[s] - state["step"] * u1[s]
                square_of = residual * residual
                a = a + square_of
                b = b + stiffness[pl.ds(table[20, s], 1), :] * square_of
            return a, b

        state["sums"] = lax.fori_loop(0, link_slots // 4, body, (nothing, nothing))

    copies = operate(1, potential_background, first_bonds, first_dots)
    gather = row.gather_begin(6, pot_all.at[1, r], pot_slot(1))
    second_bonds(copies)
    norm0, step0 = state["norm"], state["step"]
    norm_part, energy_part = state["sums"]
    for l in range(cells_dev):
        charge, value = own_cells(0, l)
        charge1, value1 = own_cells(1, l)
        energy_part = energy_part + (charge - step0 * charge1) * (value - step0 * value1)
    copies = dots_begin(1, packed(norm_part, energy_part))
    row.gather_relay(6, gather, pot_slot(1))
    copies = dots_middle(1, copies)
    row.gather_end(gather)

    def last(s, value):
        u2[s] = value + stiffness[pl.ds(table[20, s], 1), :] * u1[s]

    to_bonds(potential(1), last)
    bonds2 = send_bonds(2, u2)
    norm1, energy1 = dots_end(1, copies)
    arrive(state["bonds0"])
    arrive(state["bonds1"])
    arrive(bonds2)
    gain = norm1 / norm0
    step1 = norm1 / (energy1 - gain * norm1 / step0)
    for j in range(share):
        part = slice(j * sets, (j + 1) * sets)
        total = []
        for n in range(3):
            value = bond_in[n, 0, part, :]
            for k in range(1, cols):
                value = value + bond_in[n, k, part, :]
            total.append(value)
        residual = total[0] - step0 * total[1]
        applied = total[1] - step0 * total[2]
        out_solution[j] = step0 * total[0] + step1 * (residual + gain * total[0])
        out_residual[j] = residual - step1 * (applied + gain * total[1])
    for copy in started:
        copy.wait_send()


def on_device(
    charge_drive,
    hardness,
    bond_stiffness,
    coulomb_tiles,
    tile_rows,
    tile_cols,
    tile_count,
    link_bonds,
    link_cells,
    link_ends,
    link_carry,
    link_count,
):
    rows, cols = lax.axis_size("row"), lax.axis_size("col")
    cells_dev, sets, lanes = charge_drive.shape
    tile_slots, link_slots = coulomb_tiles.shape[0], link_bonds.shape[0]
    row_bonds = bond_stiffness.shape[0]
    group_cells, row_cells = rows * cells_dev, cols * cells_dev
    share = row_bonds // cols
    block = cells_dev * sets
    f32, bf16, i32 = jnp.float32, jnp.bfloat16, jnp.int32
    vmem = pl.BlockSpec(memory_space=pltpu.VMEM)
    smem = pl.BlockSpec(memory_space=pltpu.SMEM)
    hbm = pl.BlockSpec(memory_space=pltpu.HBM)
    width = -(-max(tile_slots, link_slots, group_cells, row_bonds) // 128) * 128
    bonds = link_bonds.reshape(1, -1)
    coulomb_tiles, link_ends, link_carry, bond_stiffness, charge_drive, hardness, tile_rows, tile_cols, bonds, link_cells = (
        pltpu.with_memory_space_constraint(x, pltpu.HBM) for x in
        (coulomb_tiles, link_ends, link_carry, bond_stiffness, charge_drive, hardness,
         tile_rows.reshape(1, -1), tile_cols.reshape(1, -1), bonds, link_cells.reshape(1, -1))
    )
    chunks = 8
    table, ends_all, weight_all, cells_all, tile_parts, tile_turned = pl.pallas_call(
        functools.partial(link_kernel, rows, cols, None),
        out_shape=(
            jax.ShapeDtypeStruct((24, width), i32),
            jax.ShapeDtypeStruct((rows, *link_ends.shape), i32),
            jax.ShapeDtypeStruct((rows, link_slots, lanes), f32),
            jax.ShapeDtypeStruct((rows, 1, width), i32),
            jax.ShapeDtypeStruct((tile_slots, 2 * lanes, lanes), bf16),
            jax.ShapeDtypeStruct((tile_slots, lanes, 2 * lanes), bf16),
        ),
        in_specs=[hbm] * 2 + [vmem] * 2 + [smem] * 3 + [hbm] + [vmem] * 2 + [hbm],
        out_specs=(vmem,) * 6,
        scratch_shapes=[
            pltpu.VMEM((tile_slots, lanes, lanes), f32),
            pltpu.VMEM((8, width), i32),
            pltpu.SemaphoreType.DMA((3,)),
            pltpu.SemaphoreType.DMA((chunks,)),
            pltpu.SemaphoreType.DMA((3, rows)),
            pltpu.SemaphoreType.DMA((3, rows)),
        ],
        compiler_params=pltpu.CompilerParams(
            collective_id=1, has_side_effects=True, vmem_limit_bytes=32 << 20
        ),
    )(
        tile_rows, tile_cols, bonds, link_cells,
        tile_count, link_count, bonds, link_ends, link_carry, bond_stiffness, coulomb_tiles,
    )
    square, charge0, fixed, sums0 = pl.pallas_call(
        functools.partial(cell_kernel, rows, (cells_dev, sets, lanes, link_slots)),
        out_shape=(
            jax.ShapeDtypeStruct((cells_dev, lanes, 2 * lanes), bf16),
            jax.ShapeDtypeStruct((cells_dev, sets, lanes), f32),
            jax.ShapeDtypeStruct((cells_dev, sets, lanes), f32),
            jax.ShapeDtypeStruct((2, sets, lanes), f32),
        ),
        in_specs=[smem] + [vmem] * 3,
        out_specs=(vmem,) * 4,
        scratch_shapes=[
            pltpu.SMEM((rows * link_slots + 2 * GROUP,), i32),
            pltpu.VMEM((cells_dev, lanes + 4 * sets, lanes), f32),
        ],
        compiler_params=pltpu.CompilerParams(vmem_limit_bytes=16 << 20),
    )(
        cells_all, ends_all.reshape(rows * link_slots, *link_ends.shape[1:]),
        weight_all.reshape(rows * link_slots, lanes), charge_drive,
    )
    out = jax.ShapeDtypeStruct((share, sets, lanes), f32)
    sizes = (cells_dev, sets, lanes, tile_slots, link_slots, row_bonds)
    return pl.pallas_call(
        functools.partial(kernel, rows, cols, sizes),
        out_shape=(out, out),
        in_specs=[smem] + [hbm] * 3 + [vmem] * 2 + [hbm] * 2 + [vmem] * 4,
        out_specs=(vmem, vmem),
        scratch_shapes=[
            pltpu.VMEM(hardness.shape, f32),
            pltpu.VMEM(bond_stiffness.shape, f32),
            pltpu.VMEM(link_ends.shape, i32),
            pltpu.VMEM(link_carry.shape, i32),
            pltpu.VMEM((link_slots, lanes, lanes), bf16),
            pltpu.VMEM((link_slots, sets, lanes), f32),
            pltpu.VMEM((link_slots, sets, lanes), f32),
            pltpu.VMEM((link_slots, sets, lanes), f32),
            pltpu.VMEM((tile_slots, sets, lanes), f32),
            pltpu.VMEM((link_slots, sets, lanes), f32),
            pltpu.VMEM((rows, cells_dev, sets, lanes), f32),
            pltpu.VMEM((2, cols, block, lanes), f32),
            pltpu.VMEM((2, rows, block, lanes), f32),
            pltpu.VMEM((row_cells, 2 * sets, lanes), bf16),
            pltpu.VMEM((group_cells, 2 * sets, 2 * lanes), bf16),
            pltpu.VMEM((2, group_cells * sets, lanes), f32),
            pltpu.VMEM((2, rows, block, lanes), f32),
            pltpu.VMEM((2, row_cells * sets, lanes), f32),
            pltpu.VMEM((2, cols, block, lanes), f32),
            pltpu.VMEM((2, rows, block, lanes), f32),
            pltpu.VMEM((group_cells, 2 * sets, lanes), bf16),
            pltpu.VMEM((3, row_bonds * sets, lanes), f32),
            pltpu.VMEM((3, cols, share * sets, lanes), f32),
            pltpu.VMEM((2, rows, sets, lanes), f32),
            pltpu.VMEM((2, cols, sets, lanes), f32),
            pltpu.SemaphoreType.DMA((5,)),
            pltpu.SemaphoreType.DMA((9, rows)),
            pltpu.SemaphoreType.DMA((9, rows)),
            pltpu.SemaphoreType.DMA((9, cols)),
            pltpu.SemaphoreType.DMA((9, cols)),
        ],
        compiler_params=pltpu.CompilerParams(
            collective_id=0, has_side_effects=True, vmem_limit_bytes=32 << 20
        ),
    )(
        table, charge_drive, hardness, bond_stiffness, tile_parts, tile_turned, link_ends, link_carry,
        square, charge0, fixed, sums0,
    )


def solution(mesh):
    return jax.shard_map(
        on_device,
        mesh=mesh,
        in_specs=(
            P(("row", "col"), None, None),
            P(("row", "col"), None),
            P("row", None),
            P(("row", "col"), None, None),
            P(("row", "col")),
            P(("row", "col")),
            P(("row", "col")),
            P(("row", "col")),
            P(("row", "col")),
            P(("row", "col"), None, None),
            P(("row", "col"), None),
            P(("row", "col")),
        ),
        out_specs=(P(("row", "col"), None, None), P(("row", "col"), None, None)),
        check_vma=False,
    )
```
